32 devices in a mesh: grp: 2 (over x), row: 8 (over z, y), col: 2 (over core).
Axes of the slice: x: 2, y: 2, z: 4, core: 2. Of those that a mesh axis runs over, the one named last changes fastest.
Arguments:
- queries: bfloat16 [8192, 2048], P(('grp', 'row'), 'col'), parts along dimension 0, may hold values from -34 to 34
- keys: bfloat16 [8192, 1024], P(('grp', 'row'), 'col'), parts along dimension 0, may hold values from -34 to 34
- values: bfloat16 [8192, 1024], P(('grp', 'row'), 'col'), parts along dimension 0, may hold values from -6 to 6
- out_proj: bfloat16 [2048, 5376], P(('col', 'row'))
- post_gain: float32 [5376], P('col'), may hold values from 0.1 to 1.9
- mean_vec: float32 [5376], P('col'), may hold values from -5 to 5
- erase_in: float32 [5376, 64], P('col'), may hold values from -0.078125 to 0.078125
- erase_out: float32 [5376, 64], P('col'), may hold values from -0.375 to 0.375
Outputs:
- erased: bfloat16 [8192, 5376], P(('grp', 'row'), 'col'), parts along dimension 0
The draws below stay inside these ranges and needn't reach their ends.
There are 2 independent parts, one for each index of `grp`. The reference program is written for one: setup_inputs(seed, part) draws one part's arguments, and reference() takes and returns one part's arrays. A program takes and returns all parts, laid end to end along the dimension named above; an argument that names none is the same for every part. Nothing has to cross between parts.
All inputs are finite; a program needn't handle non-finite values.
Results may differ from the reference program's by a relative error of at most 0.012.
The reference program's roundings to bfloat16 on the way (of `q_rot`, `k_rot`, `probs` and `attended`) count: a program that leaves them out, or rounds other values in their place, can miss the bound.
Values may be sent and summed in bfloat16 or wider, within the bound.
A program may use at most 128 MiB of HBM per device.

```python
import jax
import jax.numpy as jnp
from jax import lax

D = 5376
HD = 128
HEADS = 16
KV = 8
WINDOW = 1024
RANK = 64
TOK_DEV = 512
TOKENS = 4096
N_ROW = 8


def base_field(key, shape):
    return jnp.clip(jax.random.normal(key, shape, jnp.float32), -4.0, 4.0)


def draw_queries(key, part):
    base_draw = base_field(jax.random.fold_in(key, 11), (TOKENS, HEADS, HD))
    return base_draw.reshape(TOKENS, HEADS * HD).astype(jnp.bfloat16)


def draw_keys(key, part):
    base_draw = base_field(jax.random.fold_in(key, 13), (TOKENS, KV, HD))
    return base_draw.reshape(TOKENS, KV * HD).astype(jnp.bfloat16)


def draw_out_proj(key, part):
    columns = jnp.arange(D).astype(jnp.float32)
    ramp = jnp.exp(jnp.log(3.0) * columns / D)
    base_draw = jnp.clip(jax.random.normal(jax.random.fold_in(key, 5), (HEADS * HD, D), jnp.float32), -5.0, 5.0)
    scaled = base_draw * ramp[None, :] * float(HEADS * HD) ** (-0.5) / 1.8
    return scaled.astype(jnp.bfloat16)


def shard_levels(key, extent, pieces, smallest, top_value):
    level = 1.0
    for axis_at, shards_of in pieces:
        steps = jax.random.uniform(jax.random.fold_in(jax.random.fold_in(key, 6), axis_at), (shards_of,), jnp.float32, smallest / len(pieces), top_value / len(pieces))
        level = level * jnp.repeat(jnp.exp(steps), extent[axis_at] // shards_of).reshape((-1,) + (1,) * (len(extent) - 1 - axis_at))
    return level


def centred(rng, shape, scale, reach, shards=(), kind=jnp.bfloat16):
    values = scale * jax.random.normal(rng, shape, jnp.float32)
    if shards:
        values = values * shard_levels(rng, shape, shards, -0.22, 0.18)
    return jnp.clip(values, -reach, reach).astype(kind)


def setup_inputs(seed: int = 0, part: int = 0) -> dict:
    splits = jax.random.split(jax.random.key(seed), 9)
    part_keys = jax.random.split(jax.random.fold_in(splits[8], part), 9)
    return {
        "queries": draw_queries(jax.random.fold_in(jax.random.fold_in(splits[8], part), 71), part),
        "keys": draw_keys(jax.random.fold_in(jax.random.fold_in(splits[8], part), 71), part),
        "values": centred(part_keys[2], (TOKENS, KV * HD), 1.0, 6.0, ((0, 8), (1, 2))),
        "out_proj": draw_out_proj(jax.random.fold_in(splits[8], 71), part),
        "post_gain": jnp.clip(1.0 + 0.18 * jax.random.normal(splits[4], (D,), jnp.float32), 0.1, 1.9),
        "mean_vec": centred(splits[5], (D,), 1.0, 5.0, ((0, 2),), jnp.float32),
        "erase_in": centred(splits[6], (D, RANK), D ** -0.5, 0.078125, ((0, 2),), jnp.float32),
        "erase_out": centred(splits[7], (D, RANK), (4 * RANK) ** -0.5, 0.375, ((0, 2),), jnp.float32),
    }


query_scale = 168.0 ** (-0.5)
norm_eps = 1e-06
rope_base = 10000.0

def rotate(field, positions):
    half_dim = HD // 2
    inverse = jnp.exp(-(2.0 * jnp.arange(half_dim, dtype=jnp.float32) / HD) * jnp.log(jnp.float32(rope_base)))
    angles = positions[:, None] * inverse[None, :]
    cosine = jnp.cos(angles)[:, None, :]
    sine = jnp.sin(angles)[:, None, :]
    wide = field.astype(jnp.float32)
    first = wide[..., :half_dim]
    second = wide[..., half_dim:]
    return jnp.concatenate([first * cosine - second * sine, second * cosine + first * sine], -1).astype(jnp.bfloat16)

def reference(queries, keys, values, out_proj, post_gain, mean_vec, erase_in, erase_out):
    group = HEADS // KV
    positions = jnp.arange(TOKENS).astype(jnp.float32)
    q_rot = rotate(queries.reshape(TOKENS, HEADS, HD), positions)
    k_rot = rotate(keys.reshape(TOKENS, KV, HD), positions)
    val_heads = values.reshape(TOKENS, KV, HD)
    key_padded = jnp.pad(k_rot, ((WINDOW, 0), (0, 0), (0, 0)))
    val_padded = jnp.pad(val_heads, ((WINDOW, 0), (0, 0), (0, 0)))

    def block(block_index):
        first_row = (block_index * TOK_DEV).astype(jnp.int32)
        query_block = lax.dynamic_slice_in_dim(q_rot, first_row, TOK_DEV, 0).reshape(TOK_DEV, KV, group, HD)
        key_block = lax.dynamic_slice_in_dim(key_padded, first_row, WINDOW + TOK_DEV, 0)
        val_block = lax.dynamic_slice_in_dim(val_padded, first_row, WINDOW + TOK_DEV, 0)
        scores = jnp.einsum('tkgd,skd->kgts', query_block.astype(jnp.float32), key_block.astype(jnp.float32)) * query_scale
        query_pos = first_row + jnp.arange(TOK_DEV, dtype=jnp.int32)
        key_pos = first_row - WINDOW + jnp.arange(WINDOW + TOK_DEV, dtype=jnp.int32)
        offsets = query_pos[:, None] - key_pos[None, :]
        allowed = ((key_pos >= 0)[None, :] & (offsets >= 0) & (offsets < WINDOW))[None, None]
        scores = jnp.where(allowed, scores, -1e+30)
        row_max = lax.optimization_barrier(jnp.max(scores, axis=-1, keepdims=True))
        weights = jnp.where(allowed, jnp.exp(scores - row_max), 0.0)
        probs = (weights / lax.optimization_barrier(jnp.sum(weights, axis=-1, keepdims=True))).astype(jnp.bfloat16)
        attended = jnp.einsum('kgts,skd->tkgd', probs.astype(jnp.float32), val_block.astype(jnp.float32)).astype(jnp.bfloat16)
        attended = attended.reshape(TOK_DEV, HEADS * HD)
        hidden = jnp.dot(attended, out_proj, preferred_element_type=jnp.float32)
        inv_rms = lax.rsqrt(lax.optimization_barrier(jnp.mean(hidden * hidden, axis=-1, keepdims=True)) + norm_eps)
        normed = hidden * inv_rms * post_gain[None, :]
        erase_code = jnp.dot(normed - mean_vec[None, :], erase_in, precision=lax.Precision.HIGHEST)
        return (normed - jnp.dot(erase_code, erase_out.T, precision=lax.Precision.HIGHEST)).astype(jnp.bfloat16)
    blocks = lax.map(block, jnp.arange(N_ROW, dtype=jnp.int32))
    return blocks.reshape(TOKENS, D)
```

```python
import functools
import math

import jax
import jax.numpy as jnp
import numpy as np
from jax import lax
from jax.experimental import pallas as pl
from jax.experimental.pallas import tpu as pltpu
from jax.sharding import PartitionSpec as P

HD = 128
WINDOW = 1024
MESH = pl.DeviceIdType.MESH
query_scale = 168.0 ** (-0.5)
norm_eps = 1e-06
rope_base = 10000.0
QB = 256
BIG = 1e30

CHUNKS = ((True, 384), (False, 384), (False, 384), (False, 256), (True, 256))
VIA_Z = (2, 3)
ORDER = (
    ("own", 4), ("own", 0), ("kvup", 1), ("tables",), ("kvup", 0), ("kvy", 1), ("line", 4, -1), ("line", 4, 1),
    ("kvup", 2), ("kvup", 3), ("own", 1), ("line", 4, 2), ("line", 0, -1), ("cross", 4, 0), ("kvy", 0),
    ("kvrelay", 1), ("kvy", 2), ("line", 0, 1), ("line", 0, 2), ("cross", 0, 0), ("kvrelay", 0), ("prep",),
    ("cross", 1, 0), ("rotk", 1), ("cross", 0, -1), ("cross", 0, 1), ("line", 1, 1), ("line", 0, 3), ("kvy", 3),
    ("cross", 4, 1), ("line", 4, -2), ("G", 1), ("kvrelay", 2), ("att", 1), ("kvrelay", 3), ("own", 2), ("rotk", 0),
    ("line", 4, 3), ("cross", 4, -1), ("own", 3), ("G", 0), ("att", 0), ("line", 1, 2), ("rotk", 2), ("line", 0, -2),
    ("G", 2), ("line", 1, -1), ("rotk", 3), ("att", 2), ("line", 2, 1), ("G", 3), ("line", 3, 1), ("line", 0, -3),
    ("line", 1, 3), ("line", 4, -3), ("attfwd", 1), ("att", 3), ("cross", 0, -3), ("line", 1, -2), ("attfwd", 2),
    ("cross", 4, 3), ("line", 1, -3), ("line", 2, 2), ("line", 2, -1), ("cross", 0, 2), ("attfwd", 0),
    ("cross", 4, -2), ("cross", 4, 2), ("attfwd", 3), ("line", 2, -2), ("cross", 4, -3), ("cross", 2, 0),
    ("line", 2, 3), ("line", 3, -1), ("cross", 3, 0), ("cross", 0, 3), ("cross", 0, -2), ("mm", 1), ("line", 3, 2),
    ("line", 2, -3), ("line", 3, -2), ("mm", 2), ("line", 3, -3), ("mm", 4), ("line", 3, 3), ("mm", 3), ("mm", 0),
    ("hid", 2), ("hid", 1), ("hid", 3),
)


def plain_order(n_chunk, both, nz, kvh):
    out = [("own", k) for k in range(n_chunk)]
    out += [(a, h) for h in range(kvh) for a in ("kvup", "kvy")]
    out += [("tables",), ("prep",)]
    out += [("kvrelay", h) for h in range(kvh)]
    for k in range(n_chunk):
        for d in range(1, nz):
            out += [("line", k, -d), ("line", k, d)]
        out += [("cross", k, 0)]
        if both[k]:
            out += [("cross", k, d) for e in range(1, nz) for d in (-e, e)]
    for p in range(kvh):
        out += [("rotk", p), ("G", p), ("att", p)]
    out += [("attfwd", p) for p in range(kvh)]
    out += [("mm", k) for k in range(n_chunk)]
    out += [("hid", k) for k in range(n_chunk) if not both[k]]
    return out


def split_cat(x):
    hi = x.astype(jnp.bfloat16).astype(jnp.float32)
    return jnp.concatenate([hi, x - hi], axis=0).astype(jnp.bfloat16)


def hi_lo(x):
    hi = x.astype(jnp.bfloat16)
    return hi, (x - hi.astype(jnp.float32)).astype(jnp.bfloat16)


def dot_nt(x, y):
    return lax.dot_general(x, y, (((1,), (1,)), ((), ())), preferred_element_type=jnp.float32)


def plan(n_row):
    nz = n_row // 2
    chunks = CHUNKS if nz == 4 else ((True, 384), (False, 1152))
    via_z = VIA_Z if nz == 4 else (0,)
    both = [c[0] for c in chunks]
    width = [c[1] for c in chunks]
    off, ab, aa = [], 0, 0
    for b, w in chunks:
        off.append(aa if b else ab)
        aa, ab = (aa + w, ab) if b else (aa, ab + w)
    return both, width, off, ab, aa, via_z


def kernel(n_row, d_full, n_ss, q_hbm, k_hbm, v_hbm, w_hbm, gain_ref, mean_ref, ein_ref, eout_ref, inv_ref,
           out_ref, *scratch):
    both, width, off, pair_w, both_w, via_z = plan(n_row)
    n_chunk = len(both)
    wb = scratch[:n_chunk]
    (qbuf, kbuf, vbuf, krot, att, hid, hsend, hrecv, cosb, sinb, ein_cat, eout_cat, code_acc, sq_acc,
     st_send, st_recv, loc_sem, ss_sem, wr_sem, xr_sem, cr_sem, kr_sem, ar_sem, hr_sem, st_sem) = scratch[n_chunk:]
    nz = n_row // 2
    g, r, f = lax.axis_index("grp"), lax.axis_index("row"), lax.axis_index("col")
    zz, yy = r // 2, r % 2
    has_up, has_dn = zz < nz - 1, zz > 0
    tok = qbuf.shape[0]
    half = pair_w * 2 + both_w
    kvh = kbuf.shape[0]
    heads = qbuf.shape[1] // HD
    acols = heads * HD
    per = tok // QB

    part = {"grp": g, "row": r, "col": 1 - f}
    xnb = {"grp": 1 - g, "row": r, "col": f}
    ynb = {"grp": g, "row": 2 * zz + 1 - yy, "col": f}
    up = {"grp": g, "row": r + 2, "col": f}
    dn = {"grp": g, "row": r - 2, "col": f}

    barrier = pltpu.get_barrier_semaphore()
    for nb in (part, xnb, ynb):
        pl.semaphore_signal(barrier, inc=1, device_id=nb, device_id_type=MESH)

    @pl.when(has_up)
    def _():
        pl.semaphore_signal(barrier, inc=1, device_id=up, device_id_type=MESH)

    @pl.when(has_dn)
    def _():
        pl.semaphore_signal(barrier, inc=1, device_id=dn, device_id_type=MESH)

    def own_w(k, c):
        at = c * half + (2 * pair_w + off[k] if both[k] else g * pair_w + off[k])
        return w_hbm.at[:, pl.ds(pl.multiple_of(at, 128), width[k])]

    def head_cols(h):
        return pl.ds(h * HD, HD)

    own_rows = pl.ds(2 * tok, tok)
    loc_w = [pltpu.make_async_copy(own_w(k, f), wb[k].at[f, r], loc_sem.at[k]) for k in range(n_chunk)]
    loc_k = [pltpu.make_async_copy(k_hbm.at[:, head_cols(h)], kbuf.at[h, own_rows, :], loc_sem.at[n_chunk + h])
             for h in range(kvh)]
    loc_v = [pltpu.make_async_copy(v_hbm.at[:, head_cols(h)], vbuf.at[h, own_rows, :], loc_sem.at[n_chunk + kvh + h])
             for h in range(kvh)]
    loc_q = pltpu.make_async_copy(q_hbm, qbuf, loc_sem.at[n_chunk + 2 * kvh])
    for c in loc_w + loc_k + loc_v + [loc_q]:
        c.start()

    pl.semaphore_wait(barrier, 3 + has_up.astype(jnp.int32) + has_dn.astype(jnp.int32))

    pending = []

    def send(cond, dev, ends, *args):
        i = len(pending)
        assert i < n_ss, i

        def make():
            src, dst, recv = ends(*args)
            return pltpu.make_async_remote_copy(
                src_ref=src, dst_ref=dst, send_sem=ss_sem.at[i], recv_sem=recv, device_id=dev, device_id_type=MESH)

        pending.append((cond, make))
        if cond is None:
            make().start()
        else:
            @pl.when(cond)
            def _():
                make().start()

    def when(cond, fn):
        if cond is None:
            fn()
        else:
            pl.when(cond)(fn)

    def arrived(ref, sem):
        pltpu.make_async_copy(ref, ref, sem).wait()

    for k in range(n_chunk):
        send(None, part, lambda k: (own_w(k, 1 - f), wb[k].at[f, r], cr_sem.at[k]), k)

    def block(k, u):
        return wb[k].at[g, u] if both[k] else wb[k].at[:, u]

    def send_w(cond, k, u, dev):
        send(cond, dev, lambda: (block(k, u), block(k, u), wr_sem.at[k, u]))

    def send_x(cond, k, u):
        send(cond, xnb, lambda: (wb[k].at[g, u], wb[k].at[g, u], xr_sem.at[k, u]))

    def act_own(k):
        loc_w[k].wait()
        arrived(wb[k].at[1 - f, r], cr_sem.at[k])
        send_w(has_up, k, r, up)
        send_w(has_dn, k, r, dn)
        send_w(None, k, r, ynb)

    def inside(dz):
        return None if dz == 0 else (zz + dz >= 0 if dz < 0 else zz + dz < nz)

    def act_line(k, dz):
        cond, u = inside(dz), r + 2 * dz
        when(cond, lambda: arrived(block(k, u), wr_sem.at[k, u]))
        if dz < 0:
            send_w(cond & has_up, k, u, up)
        else:
            send_w(cond & has_dn, k, u, dn)
        if dz != 1:
            send_w(cond & has_up if dz == -1 and k in via_z else cond, k, u, ynb)
        if both[k]:
            send_x(cond, k, u)

    def act_cross(k, dz):
        cond, u = inside(dz), 2 * (zz + dz) + 1 - yy
        when(cond, lambda: arrived(block(k, u), wr_sem.at[k, u]))
        if dz == 0:
            send_w(has_dn, k, u, dn)
            if k in via_z:
                send_w(zz == nz - 2, k, u, up)
        if both[k]:
            send_x(cond, k, u)

    def kv_rows(slot):
        return pl.ds(slot * tok, tok)

    def send_kv(cond, h, src_slot, slot, dev):
        def ends(n):
            hbm, buf = ((k_hbm, kbuf), (v_hbm, vbuf))[n]
            src = hbm.at[:, head_cols(h)] if src_slot == 2 else buf.at[h, kv_rows(src_slot), :]
            return src, buf.at[h, kv_rows(slot), :], kr_sem.at[slot, h, n]

        for n in range(2):
            send(cond, dev, ends, n)

    def wait_kv(cond, h, slot):
        @pl.when(cond)
        def _():
            for n, buf in enumerate((kbuf, vbuf)):
                arrived(buf.at[h, kv_rows(slot), :], kr_sem.at[slot, h, n])

    def act_kvup(h):
        send_kv(has_up, h, 2, 0, up)

    def act_kvy(h):
        send_kv(yy == 0, h, 2, 1, ynb)

    def act_kvrelay(h):
        wait_kv(has_dn, h, 0)
        send_kv(has_dn & (yy == 1), h, 0, 1, ynb)

    sign = jnp.where(lax.broadcasted_iota(jnp.int32, (1, HD), 1) < HD // 2, -1.0, 1.0)
    key_base = r * tok - 2 * tok

    def table(i, _):
        at = pl.multiple_of(i * 128, 128)
        pos = (key_base + at + lax.broadcasted_iota(jnp.int32, (128, HD), 0)).astype(jnp.float32)
        ang = pos * inv_ref[...]
        cosb[pl.ds(at, 128), :] = jnp.cos(ang)
        sinb[pl.ds(at, 128), :] = jnp.sin(ang) * sign
        return 0

    def turned(x, at):
        x = x.astype(jnp.float32)
        cs, sn = cosb[pl.ds(at, 128), :], sinb[pl.ds(at, 128), :]
        return (x * cs + pltpu.roll(x, HD // 2, 1) * sn).astype(jnp.bfloat16)

    def rot_q(i, _):
        at = pl.multiple_of(i * 128, 128)
        for h in range(heads):
            cols = slice(h * HD, (h + 1) * HD)
            qbuf[pl.ds(at, 128), cols] = turned(qbuf[pl.ds(at, 128), cols], 2 * tok + at)
        return 0

    def rot_own(i, _):
        at = pl.multiple_of(2 * tok + i * 128, 128)
        for h in range(kvh):
            krot[h, pl.ds(at, 128), :] = turned(kbuf[h, pl.ds(at, 128), :], at)
        return 0

    def act_tables():
        @pl.when(zz == 0)
        def _():
            kbuf[:, kv_rows(0), :] = jnp.zeros((kvh, tok, HD), kbuf.dtype)
            vbuf[:, kv_rows(0), :] = jnp.zeros((kvh, tok, HD), vbuf.dtype)

        @pl.when(r == 0)
        def _():
            kbuf[:, kv_rows(1), :] = jnp.zeros((kvh, tok, HD), kbuf.dtype)
            vbuf[:, kv_rows(1), :] = jnp.zeros((kvh, tok, HD), vbuf.dtype)

        lax.fori_loop(0, 3 * tok // 128, table, 0)

    def prep(i, _):
        cols = pl.ds(pl.multiple_of(i * 384, 128), 384)
        ein_cat[:, cols] = split_cat(ein_ref[:, cols])
        eout_cat[:, cols] = split_cat(eout_ref[:, cols])
        return 0

    def act_prep():
        loc_q.wait()
        lax.fori_loop(0, tok // 128, rot_q, 0)
        for c in loc_k + loc_v:
            c.wait()
        lax.fori_loop(0, tok // 128, rot_own, 0)
        lax.fori_loop(0, half // 384, prep, 0)
        m_hi, m_lo = hi_lo(jnp.broadcast_to(mean_ref[...][None, :], (16, half)))
        m_acc = dot_nt(m_hi, ein_cat[...]) + dot_nt(m_lo, ein_cat[...])
        st_send[tok:tok + 8, :] = (m_acc + pltpu.roll(m_acc, HD // 2, 1))[0:8]
        code_acc[...] = jnp.zeros_like(code_acc)
        sq_acc[...] = jnp.zeros_like(sq_acc)

    def act_rotk(h):
        wait_kv(r > 0, h, 1)

        def body(i, _):
            at = pl.multiple_of(i * 128, 128)
            krot[h, pl.ds(at, 128), :] = turned(kbuf[h, pl.ds(at, 128), :], at)
            return 0

        lax.fori_loop(0, 2 * tok // 128, body, 0)

    nt = WINDOW // QB + 1
    ri = lax.broadcasted_iota(jnp.int32, (QB, QB), 0)
    ci = lax.broadcasted_iota(jnp.int32, (QB, QB), 1)
    pen = [jnp.where(zz > 0, 0.0, BIG), jnp.where(r > 0, 0.0, BIG), jnp.float32(0.0)]

    def act_G(kv):
        def piece(j, _):
            head, i = (heads // kvh) * kv + j // per, j % per
            rows = pl.ds(pl.multiple_of(i * QB, QB), QB)
            qt = qbuf[rows, pl.ds(pl.multiple_of(head * HD, HD), HD)]
            key_rows = pl.ds(pl.multiple_of(i * QB, QB), nt * QB)
            s = dot_nt(qt, krot[kv, key_rows, :]) * query_scale
            tiles, bias, m = [], [], None
            for t in range(nt):
                st = s[:, t * QB:(t + 1) * QB]
                if t == 0:
                    st = jnp.where(ci > ri, st, -BIG)
                if t == nt - 1:
                    st = jnp.where(ci <= ri, st, -BIG)
                blk = (i + t) // per
                b = jnp.where(blk == 0, pen[0], jnp.where(blk == 1, pen[1], pen[2]))
                mt = jnp.max(st, axis=1, keepdims=True) - b
                m = mt if m is None else jnp.maximum(m, mt)
                tiles.append(st)
                bias.append(b)
            es, tot = [], None
            for st, b in zip(tiles, bias):
                e = jnp.exp(st - (m + b))
                es.append(e)
                se = jnp.sum(e, axis=1, keepdims=True)
                tot = se if tot is None else tot + se
            inv = 1.0 / tot
            p = jnp.concatenate([(e * inv).astype(jnp.bfloat16) for e in es], axis=1)
            o = jnp.dot(p, vbuf[kv, key_rows, :], preferred_element_type=jnp.float32)
            att[rows, pl.ds(pl.multiple_of(f * acols + head * HD, HD), HD)] = o.astype(jnp.bfloat16)
            return 0

        lax.fori_loop(0, (heads // kvh) * per, piece, 0)

    group = heads // kvh * HD
    mine, other = pl.ds(0, tok), pl.ds(tok, tok)

    def att_cols(c, p):
        return pl.ds(pl.multiple_of(c * acols + p * group, 128), group)

    def act_att(p):
        cols = att_cols(f, p)
        send(None, xnb, lambda: (att.at[mine, cols], att.at[other, cols], ar_sem.at[0, p]))
        send(None, part, lambda: (att.at[mine, cols], att.at[mine, cols], ar_sem.at[1, p]))

    def act_attfwd(p):
        cols = att_cols(f, p)
        arrived(att.at[other, cols], ar_sem.at[0, p])
        send(None, part, lambda: (att.at[other, cols], att.at[other, cols], ar_sem.at[2, p]))

    lane = lax.broadcasted_iota(jnp.int32, (tok, HD), 1)
    gained = [False, False]

    def stats(src, at, out_at, w):
        def body(i, _):
            rows = pl.ds(pl.multiple_of(i * 128, 128), 128)
            h = src[rows, pl.ds(at, w)].astype(jnp.float32)
            cols = pl.ds(out_at if isinstance(out_at, int) else pl.multiple_of(out_at, 128), w)
            hg_hi, hg_lo = hi_lo(h * gain_ref[cols][None, :])
            e = ein_cat[:, cols]
            code_acc[rows, :] += dot_nt(hg_hi, e) + dot_nt(hg_lo, e)
            sq = sq_acc[rows, :]
            for t in range(w // HD):
                ht = h[:, t * HD:(t + 1) * HD]
                sq = sq + ht * ht
            sq_acc[rows, :] = sq
            return 0

        lax.fori_loop(0, tok // 128, body, 0)

    def act_mm(k):
        if not gained[0]:
            gained[0] = True
            for p in range(kvh):
                arrived(att.at[mine, att_cols(1 - f, p)], ar_sem.at[1, p])
        if both[k]:
            for dz in range(1 - nz, nz):
                for u, skip in ((r + 2 * dz, dz == 0), (2 * (zz + dz) + 1 - yy, False)):
                    if not skip:
                        when(inside(dz), lambda: arrived(wb[k].at[1 - g, u], xr_sem.at[k, u]))
        else:
            if not gained[1]:
                gained[1] = True
                for p in range(kvh):
                    arrived(att.at[other, att_cols(1 - f, p)], ar_sem.at[2, p])
            for dz in range(1 - nz, nz):
                if dz != 0:
                    act_cross(k, dz)
        wk = wb[k].reshape(2 * acols, width[k])

        def product(at):
            return jnp.dot(att[pl.ds(pl.multiple_of(at, QB), QB), :], wk[...], preferred_element_type=jnp.float32)

        if both[k]:
            def body(i, _):
                at = pl.multiple_of(i * QB, QB)
                hid[pl.ds(at, QB), pair_w + off[k]:pair_w + off[k] + width[k]] = product(at)
                return 0

            lax.fori_loop(0, per, body, 0)
            stats(hid, pair_w + off[k], 2 * pair_w + off[k], width[k])
        else:
            cols = slice(off[k], off[k] + width[k])

            def body(i, _):
                n = jnp.where(i < per, i, i - per)
                at = pl.multiple_of(n * QB, QB)
                d = product(jnp.where(i < per, tok, 0) + at)

                @pl.when(i < per)
                def _():
                    hsend[pl.ds(at, QB), cols] = d.astype(jnp.bfloat16)

                def ends(j):
                    rows = pl.ds(j * QB, QB)
                    return hsend.at[rows, cols], hrecv.at[rows, cols], hr_sem.at[k, j]

                for j in range(per):
                    send(i == j, xnb, ends, j)
                    pending[-1] = (None, pending[-1][1])

                @pl.when(i >= per)
                def _():
                    hid[pl.ds(at, QB), cols] = d
                return 0

            lax.fori_loop(0, 2 * per, body, 0)
            stats(hid, off[k], g * pair_w + off[k], width[k])

    def act_hid(k):
        cols = slice(off[k], off[k] + width[k])
        for j in range(per):
            arrived(hrecv.at[pl.ds(j * QB, QB), cols], hr_sem.at[k, j])
        stats(hrecv, off[k], (1 - g) * pair_w + off[k], width[k])

    acts = {"own": act_own, "line": act_line, "cross": act_cross, "kvup": act_kvup, "kvy": act_kvy,
            "kvrelay": act_kvrelay, "tables": act_tables, "prep": act_prep, "rotk": act_rotk, "G": act_G,
            "att": act_att, "attfwd": act_attfwd, "mm": act_mm, "hid": act_hid}
    for name, *rest in ORDER if nz == 4 else plain_order(n_chunk, both, nz, kvh):
        acts[name](*rest)

    code = code_acc[...]
    code = code + pltpu.roll(code, HD // 2, 1)
    sq = jnp.sum(sq_acc[...], axis=1, keepdims=True)
    st_send[0:tok, :] = jnp.where(lane < HD // 2, code, sq)
    swap = pltpu.make_async_remote_copy(src_ref=st_send, dst_ref=st_recv, send_sem=st_sem.at[0], recv_sem=st_sem.at[1],
                                        device_id=part, device_id_type=MESH)
    swap.start()
    for cond, make in pending:
        when(cond, lambda make=make: make().wait_send())
    swap.wait()
    sums = st_send[0:tok, :] + st_recv[0:tok, :]
    turned_sums = pltpu.roll(sums, HD // 2, 1)
    code = jnp.where(lane < HD // 2, sums, turned_sums)
    total = jnp.where(lane < HD // 2, turned_sums, sums)
    inv_rms = lax.rsqrt(total * (1.0 / d_full) + norm_eps)
    mean_sum = st_send[tok:tok + 1, :] + st_recv[tok:tok + 1, :]
    c_hi, c_lo = hi_lo(inv_rms * code - mean_sum)
    scale = inv_rms[:, 0:1]

    def finish(src, at, out_at, w):
        step = math.gcd(w, 384)

        def body(n, _):
            cols = pl.ds(pl.multiple_of(at + n * step, 128), step)
            to = pl.ds(pl.multiple_of(out_at + n * step, 128), step)
            e = eout_cat[:, to]
            back = jnp.dot(c_hi, e, preferred_element_type=jnp.float32) + jnp.dot(
                c_lo, e, preferred_element_type=jnp.float32)
            h = src[:, cols].astype(jnp.float32)
            out_ref[:, to] = (h * scale * gain_ref[to][None, :] - back).astype(jnp.bfloat16)
            return 0

        lax.fori_loop(0, w // step, body, 0)

    finish(hid, 0, g * pair_w, pair_w)
    finish(hrecv, 0, (1 - g) * pair_w, pair_w)
    finish(hid, pair_w, 2 * pair_w, both_w)


def solution(mesh):
    n_row = mesh.shape["row"]

    def on_device(queries, keys, values, out_proj, post_gain, mean_vec, erase_in, erase_out):
        tok = queries.shape[0]
        rows, d_full = out_proj.shape
        half = post_gain.shape[0]
        half_dim = HD // 2
        kvh = keys.shape[1] // HD
        inverse = np.exp(-(2.0 * np.arange(half_dim, dtype=np.float32) / HD) * np.log(np.float32(rope_base)))
        inverse = np.concatenate([inverse, inverse]).astype(np.float32)[None, :]
        any_spec = pl.BlockSpec(memory_space=pl.ANY)
        vm = pl.BlockSpec(memory_space=pltpu.VMEM)
        both, width, off, pair_w, both_w, via_z = plan(n_row)
        n_chunk = len(both)
        hops = n_row // 2 - 1
        n_ss = sum(6 + 4 * hops + b * (4 * hops + 1) + tok // QB for b in both) + 9 * kvh
        bf, f32 = jnp.bfloat16, jnp.float32
        dma = pltpu.SemaphoreType.DMA
        return pl.pallas_call(
            functools.partial(kernel, n_row, d_full, n_ss),
            out_shape=jax.ShapeDtypeStruct((tok, half), bf),
            in_specs=[any_spec] * 4 + [vm] * 5,
            out_specs=vm,
            scratch_shapes=[pltpu.VMEM((2, n_row, rows, w), bf) for w in width] + [
                pltpu.VMEM(queries.shape, bf),
                pltpu.VMEM((kvh, 3 * tok, HD), bf),
                pltpu.VMEM((kvh, 3 * tok, HD), bf),
                pltpu.VMEM((kvh, 3 * tok, HD), bf),
                pltpu.VMEM((2 * tok, 2 * queries.shape[1]), bf),
                pltpu.VMEM((tok, pair_w + both_w), f32),
                pltpu.VMEM((tok, pair_w), bf),
                pltpu.VMEM((tok, pair_w), bf),
                pltpu.VMEM((3 * tok, HD), f32),
                pltpu.VMEM((3 * tok, HD), f32),
                pltpu.VMEM((HD, half), bf),
                pltpu.VMEM((HD, half), bf),
                pltpu.VMEM((tok, HD), f32),
                pltpu.VMEM((tok, HD), f32),
                pltpu.VMEM((tok + 8, HD), f32),
                pltpu.VMEM((tok + 8, HD), f32),
                dma((n_chunk + 2 * kvh + 1,)), dma((n_ss,)), dma((n_chunk, n_row)), dma((n_chunk, n_row)),
                dma((n_chunk,)), dma((2, kvh, 2)), dma((3, kvh)), dma((n_chunk, tok // QB)), dma((2,)),
            ],
            compiler_params=pltpu.CompilerParams(
                collective_id=0, has_side_effects=True, vmem_limit_bytes=60 * 1024 * 1024),
        )(queries, keys, values, out_proj, post_gain, mean_vec,
          erase_in.T, erase_out.T, jnp.asarray(inverse))

    placed = (
        P(("grp", "row"), "col"),
        P(("grp", "row"), "col"),
        P(("grp", "row"), "col"),
        P(("col", "row"), None),
        P("col"),
        P("col"),
        P("col", None),
        P("col", None),
    )
    return jax.shard_map(
        on_device, mesh=mesh, in_specs=placed, out_specs=P(("grp", "row"), "col"), check_vma=False
    )
```

```python
import functools

import jax
import jax.numpy as jnp
import numpy as np
from jax import lax
from jax.experimental import pallas as pl
from jax.experimental.pallas import tpu as pltpu
from jax.sharding import PartitionSpec as P

HD = 128
WINDOW = 1024
MESH = pl.DeviceIdType.MESH
query_scale = 168.0 ** (-0.5)
norm_eps = 1e-06
rope_base = 10000.0
QB = 256
TN = 384
BIG = 1e30

CHUNKS = ((True, 512), (False, 384), (False, 384), (False, 256), (True, 128))
VIA_Z = (2, 3)
ORDER = (
    ("kvup", 1), ("own", 4), ("kvup", 0), ("kvy", 1), ("kvup", 3), ("own", 0), ("kvup", 2), ("own", 2), ("tables",),
    ("line", 0, 1), ("cross", 4, 0), ("prep",), ("kvrelay", 1), ("cross", 0, 0), ("line", 4, 1), ("line", 0, 2),
    ("kvrelay", 0), ("kvy", 0), ("cross", 4, 1), ("kvy", 3), ("line", 4, -1), ("line", 2, 1), ("rotk", 1), ("G", 1),
    ("att", 1), ("line", 0, 3), ("kvrelay", 3), ("rotk", 0), ("line", 0, -1), ("G", 0), ("att", 0), ("rotk", 3),
    ("kvrelay", 2), ("kvy", 2), ("own", 1), ("G", 3), ("att", 3), ("cross", 0, 3), ("line", 1, 1), ("line", 0, -2),
    ("line", 4, 2), ("rotk", 2), ("line", 1, 2), ("line", 1, -1), ("cross", 0, -1), ("line", 4, -2), ("cross", 0, 2),
    ("line", 2, 2), ("G", 2), ("att", 2), ("line", 1, -2), ("line", 0, -3), ("cross", 4, -1), ("cross", 4, 2),
    ("line", 4, 3), ("line", 1, 3), ("cross", 1, 0), ("own", 3), ("line", 2, -1), ("line", 4, -3), ("cross", 0, 1),
    ("cross", 4, 3), ("line", 1, -3), ("cross", 0, -2), ("line", 2, -2), ("attfwd", 1), ("cross", 4, -2),
    ("attfwd", 3), ("attfwd", 0), ("cross", 4, -3), ("attfwd", 2), ("line", 2, 3), ("line", 3, -1), ("line", 3, 1),
    ("cross", 0, -3), ("cross", 2, 0), ("line", 2, -3), ("mm", 1), ("line", 3, 2), ("line", 3, -2), ("mm", 0),
    ("cross", 3, 0), ("mm", 2), ("line", 3, -3), ("hid", 1), ("line", 3, 3), ("mm", 3), ("hid", 2), ("mm", 4),
    ("hid", 3),
)


def plain_order(n_chunk, both, nz, kvh):
    out = [("own", k) for k in range(n_chunk)]
    out += [(a, h) for h in range(kvh) for a in ("kvup", "kvy")]
    out += [("tables",), ("prep",)]
    out += [("kvrelay", h) for h in range(kvh)]
    for k in range(n_chunk):
        for d in range(1, nz):
            out += [("line", k, -d), ("line", k, d)]
        out += [("cross", k, 0)]
        if both[k]:
            out += [("cross", k, d) for e in range(1, nz) for d in (-e, e)]
    for p in range(kvh):
        out += [("rotk", p), ("G", p), ("att", p)]
    out += [("attfwd", p) for p in range(kvh)]
    out += [("mm", k) for k in range(n_chunk)]
    out += [("hid", k) for k in range(n_chunk) if not both[k]]
    return out


def split_cat(x):
    hi = x.astype(jnp.bfloat16).astype(jnp.float32)
    return jnp.concatenate([hi, x - hi], axis=0).astype(jnp.bfloat16)


def hi_lo(x):
    hi = x.astype(jnp.bfloat16)
    return hi, (x - hi.astype(jnp.float32)).astype(jnp.bfloat16)


def dot_nt(x, y):
    return lax.dot_general(x, y, (((1,), (1,)), ((), ())), preferred_element_type=jnp.float32)


def plan(n_row):
    nz = n_row // 2
    chunks = CHUNKS if nz == 4 else ((True, 384), (False, 1152))
    via_z = VIA_Z if nz == 4 else (0,)
    both = [c[0] for c in chunks]
    width = [c[1] for c in chunks]
    off, ab, aa = [], 0, 0
    for b, w in chunks:
        off.append(aa if b else ab)
        aa, ab = (aa + w, ab) if b else (aa, ab + w)
    return both, width, off, ab, aa, via_z


def kernel(n_row, d_full, n_ss, q_hbm, k_hbm, v_hbm, w_hbm, *rest):
    params_hbm, rest = rest[:5], rest[5:]
    hid_out, eout_out, c_ref, scale_ref, *scratch = rest
    both, width, off, pair_w, both_w, via_z = plan(n_row)
    n_chunk = len(both)
    wb = scratch[:n_chunk]
    (qbuf, kbuf, vbuf, krot, att, hid, hsend, cosb, sinb, ein_cat, eout_cat, code_acc, sq_acc, st_send, st_recv,
     gain_ref, mean_ref, ein_ref, eout_ref, inv_ref, loc_sem, ss_sem, wr_sem, xr_sem, cr_sem, kr_sem, ar_sem, hr_sem, st_sem, out_sem) = scratch[n_chunk:]
    nz = n_row // 2
    g, r, f = lax.axis_index("grp"), lax.axis_index("row"), lax.axis_index("col")
    zz, yy = r // 2, r % 2
    has_up, has_dn = zz < nz - 1, zz > 0
    tok = qbuf.shape[0]
    half = pair_w * 2 + both_w
    kvh = kbuf.shape[0]
    heads = qbuf.shape[1] // HD
    acols = heads * HD
    per = tok // QB

    part = {"grp": g, "row": r, "col": 1 - f}
    xnb = {"grp": 1 - g, "row": r, "col": f}
    ynb = {"grp": g, "row": 2 * zz + 1 - yy, "col": f}
    up = {"grp": g, "row": r + 2, "col": f}
    dn = {"grp": g, "row": r - 2, "col": f}

    barrier = pltpu.get_barrier_semaphore()
    for nb in (part, xnb, ynb):
        pl.semaphore_signal(barrier, inc=1, device_id=nb, device_id_type=MESH)

    @pl.when(has_up)
    def _():
        pl.semaphore_signal(barrier, inc=1, device_id=up, device_id_type=MESH)

    @pl.when(has_dn)
    def _():
        pl.semaphore_signal(barrier, inc=1, device_id=dn, device_id_type=MESH)

    def own_w(k, c):
        at = c * half + (2 * pair_w + off[k] if both[k] else g * pair_w + off[k])
        return w_hbm.at[:, pl.ds(pl.multiple_of(at, 128), width[k])]

    def head_cols(h):
        return pl.ds(h * HD, HD)

    own_rows = pl.ds(2 * tok, tok)
    loc_w = [pltpu.make_async_copy(own_w(k, f), wb[k].at[f, r], loc_sem.at[k]) for k in range(n_chunk)]
    loc_k = [pltpu.make_async_copy(k_hbm.at[:, head_cols(h)], kbuf.at[h, own_rows, :], loc_sem.at[n_chunk + h])
             for h in range(kvh)]
    loc_v = [pltpu.make_async_copy(v_hbm.at[:, head_cols(h)], vbuf.at[h, own_rows, :], loc_sem.at[n_chunk + kvh + h])
             for h in range(kvh)]
    loc_q = pltpu.make_async_copy(q_hbm, qbuf, loc_sem.at[n_chunk + 2 * kvh])
    loc_p = [pltpu.make_async_copy(src, dst, loc_sem.at[n_chunk + 2 * kvh + 1 + i]) for i, (src, dst) in enumerate(
        zip(params_hbm, (gain_ref, mean_ref, ein_ref, eout_ref, inv_ref)))]
    for c in loc_w + loc_k + loc_v + [loc_q] + loc_p:
        c.start()

    pl.semaphore_wait(barrier, 3 + has_up.astype(jnp.int32) + has_dn.astype(jnp.int32))

    pending = []
    left = []

    def leave(src, dst):
        c = pltpu.make_async_copy(src, dst, out_sem.at[len(left)])
        left.append(c)
        c.start()

    def send(cond, dev, ends, *args):
        i = len(pending)
        assert i < n_ss, i

        def make():
            src, dst, recv = ends(*args)
            return pltpu.make_async_remote_copy(
                src_ref=src, dst_ref=dst, send_sem=ss_sem.at[i], recv_sem=recv, device_id=dev, device_id_type=MESH)

        pending.append((cond, make))
        if cond is None:
            make().start()
        else:
            @pl.when(cond)
            def _():
                make().start()

    def when(cond, fn):
        if cond is None:
            fn()
        else:
            pl.when(cond)(fn)

    def arrived(ref, sem):
        pltpu.make_async_copy(ref, ref, sem).wait()

    for k in range(n_chunk):
        send(None, part, lambda k: (own_w(k, 1 - f), wb[k].at[f, r], cr_sem.at[k]), k)

    def block(k, u):
        return wb[k].at[g, u] if both[k] else wb[k].at[:, u]

    def send_w(cond, k, u, dev):
        send(cond, dev, lambda: (block(k, u), block(k, u), wr_sem.at[k, u]))

    def send_x(cond, k, u):
        send(cond, xnb, lambda: (wb[k].at[g, u], wb[k].at[g, u], xr_sem.at[k, u]))

    def act_own(k):
        loc_w[k].wait()
        arrived(wb[k].at[1 - f, r], cr_sem.at[k])
        send_w(has_up, k, r, up)
        send_w(has_dn, k, r, dn)
        send_w(None, k, r, ynb)

    def inside(dz):
        return None if dz == 0 else (zz + dz >= 0 if dz < 0 else zz + dz < nz)

    def act_line(k, dz):
        cond, u = inside(dz), r + 2 * dz
        when(cond, lambda: arrived(block(k, u), wr_sem.at[k, u]))
        if dz < 0:
            send_w(cond & has_up, k, u, up)
        else:
            send_w(cond & has_dn, k, u, dn)
        if dz != 1:
            send_w(cond & has_up if dz == -1 and k in via_z else cond, k, u, ynb)
        if both[k]:
            send_x(cond, k, u)

    def act_cross(k, dz):
        cond, u = inside(dz), 2 * (zz + dz) + 1 - yy
        when(cond, lambda: arrived(block(k, u), wr_sem.at[k, u]))
        if dz == 0:
            send_w(has_dn, k, u, dn)
            if k in via_z:
                send_w(zz == nz - 2, k, u, up)
        if both[k]:
            send_x(cond, k, u)

    def kv_rows(slot):
        return pl.ds(slot * tok, tok)

    def send_kv(cond, h, src_slot, slot, dev):
        def ends(n):
            hbm, buf = ((k_hbm, kbuf), (v_hbm, vbuf))[n]
            src = hbm.at[:, head_cols(h)] if src_slot == 2 else buf.at[h, kv_rows(src_slot), :]
            return src, buf.at[h, kv_rows(slot), :], kr_sem.at[slot, h, n]

        for n in range(2):
            send(cond, dev, ends, n)

    def wait_kv(cond, h, slot):
        @pl.when(cond)
        def _():
            for n, buf in enumerate((kbuf, vbuf)):
                arrived(buf.at[h, kv_rows(slot), :], kr_sem.at[slot, h, n])

    def act_kvup(h):
        send_kv(has_up, h, 2, 0, up)

    def act_kvy(h):
        send_kv(yy == 0, h, 2, 1, ynb)

    def act_kvrelay(h):
        wait_kv(has_dn, h, 0)
        send_kv(has_dn & (yy == 1), h, 0, 1, ynb)

    sign = jnp.where(lax.broadcasted_iota(jnp.int32, (1, HD), 1) < HD // 2, -1.0, 1.0)
    key_base = r * tok - 2 * tok

    def table(i, _):
        at = pl.multiple_of(i * 128, 128)
        pos = (key_base + at + lax.broadcasted_iota(jnp.int32, (128, HD), 0)).astype(jnp.float32)
        ang = pos * inv_ref[...]
        cosb[pl.ds(at, 128), :] = jnp.cos(ang)
        sinb[pl.ds(at, 128), :] = jnp.sin(ang) * sign
        return 0

    def turned(x, at):
        x = x.astype(jnp.float32)
        cs, sn = cosb[pl.ds(at, 128), :], sinb[pl.ds(at, 128), :]
        return (x * cs + pltpu.roll(x, HD // 2, 1) * sn).astype(jnp.bfloat16)

    def rot_q(i, _):
        at = pl.multiple_of(i * 128, 128)
        for h in range(heads):
            cols = slice(h * HD, (h + 1) * HD)
            qbuf[pl.ds(at, 128), cols] = turned(qbuf[pl.ds(at, 128), cols], 2 * tok + at)
        return 0

    def rot_own(i, _):
        at = pl.multiple_of(2 * tok + i * 128, 128)
        for h in range(kvh):
            krot[h, pl.ds(at, 128), :] = turned(kbuf[h, pl.ds(at, 128), :], at)
        return 0

    def act_tables():
        @pl.when(zz == 0)
        def _():
            kbuf[:, kv_rows(0), :] = jnp.zeros((kvh, tok, HD), kbuf.dtype)
            vbuf[:, kv_rows(0), :] = jnp.zeros((kvh, tok, HD), vbuf.dtype)

        @pl.when(r == 0)
        def _():
            kbuf[:, kv_rows(1), :] = jnp.zeros((kvh, tok, HD), kbuf.dtype)
            vbuf[:, kv_rows(1), :] = jnp.zeros((kvh, tok, HD), vbuf.dtype)

        for c in loc_p:
            c.wait()
        lax.fori_loop(0, 3 * tok // 128, table, 0)

    def prep(i, _):
        cols = pl.ds(pl.multiple_of(i * 384, 128), 384)
        ein_cat[:, cols] = split_cat(ein_ref[:, cols])
        eout_cat[:, cols] = split_cat(eout_ref[:, cols])
        return 0

    def act_prep():
        loc_q.wait()
        lax.fori_loop(0, tok // 128, rot_q, 0)
        for c in loc_k + loc_v:
            c.wait()
        lax.fori_loop(0, tok // 128, rot_own, 0)
        lax.fori_loop(0, half // 384, prep, 0)
        leave(eout_cat, eout_out)
        m_hi, m_lo = hi_lo(jnp.broadcast_to(mean_ref[...][None, :], (16, half)))
        m_acc = dot_nt(m_hi, ein_cat[...]) + dot_nt(m_lo, ein_cat[...])
        st_send[tok:tok + 8, :] = (m_acc + pltpu.roll(m_acc, HD // 2, 1))[0:8]
        code_acc[...] = jnp.zeros_like(code_acc)
        sq_acc[...] = jnp.zeros_like(sq_acc)

    def act_rotk(h):
        wait_kv(r > 0, h, 1)

        def body(i, _):
            at = pl.multiple_of(i * 128, 128)
            krot[h, pl.ds(at, 128), :] = turned(kbuf[h, pl.ds(at, 128), :], at)
            return 0

        lax.fori_loop(0, 2 * tok // 128, body, 0)

    nt = WINDOW // QB + 1
    ri = lax.broadcasted_iota(jnp.int32, (QB, QB), 0)
    ci = lax.broadcasted_iota(jnp.int32, (QB, QB), 1)
    pen = [jnp.where(zz > 0, 0.0, BIG), jnp.where(r > 0, 0.0, BIG), jnp.float32(0.0)]

    def act_G(kv):
        def piece(j, _):
            head, i = (heads // kvh) * kv + j // per, j % per
            rows = pl.ds(pl.multiple_of(i * QB, QB), QB)
            qt = qbuf[rows, pl.ds(pl.multiple_of(head * HD, HD), HD)]
            key_rows = pl.ds(pl.multiple_of(i * QB, QB), nt * QB)
            s = dot_nt(qt, krot[kv, key_rows, :]) * query_scale
            tiles, bias, m = [], [], None
            for t in range(nt):
                st = s[:, t * QB:(t + 1) * QB]
                if t == 0:
                    st = jnp.where(ci > ri, st, -BIG)
                if t == nt - 1:
                    st = jnp.where(ci <= ri, st, -BIG)
                blk = (i + t) // per
                b = jnp.where(blk == 0, pen[0], jnp.where(blk == 1, pen[1], pen[2]))
                mt = jnp.max(st, axis=1, keepdims=True) - b
                m = mt if m is None else jnp.maximum(m, mt)
                tiles.append(st)
                bias.append(b)
            es, tot = [], None
            for st, b in zip(tiles, bias):
                e = jnp.exp(st - (m + b))
                es.append(e)
                se = jnp.sum(e, axis=1, keepdims=True)
                tot = se if tot is None else tot + se
            inv = 1.0 / tot
            p = jnp.concatenate([(e * inv).astype(jnp.bfloat16) for e in es], axis=1)
            o = jnp.dot(p, vbuf[kv, key_rows, :], preferred_element_type=jnp.float32)
            att[rows, pl.ds(pl.multiple_of(f * acols + head * HD, HD), HD)] = o.astype(jnp.bfloat16)
            return 0

        lax.fori_loop(0, (heads // kvh) * per, piece, 0)

    group = heads // kvh * HD
    mine, other = pl.ds(0, tok), pl.ds(tok, tok)

    def att_cols(c, p):
        return pl.ds(pl.multiple_of(c * acols + p * group, 128), group)

    def act_att(p):
        cols = att_cols(f, p)
        send(None, xnb, lambda: (att.at[mine, cols], att.at[other, cols], ar_sem.at[0, p]))
        send(None, part, lambda: (att.at[mine, cols], att.at[mine, cols], ar_sem.at[1, p]))

    def act_attfwd(p):
        cols = att_cols(f, p)
        arrived(att.at[other, cols], ar_sem.at[0, p])
        send(None, part, lambda: (att.at[other, cols], att.at[other, cols], ar_sem.at[2, p]))

    lane = lax.broadcasted_iota(jnp.int32, (tok, HD), 1)
    gained = [False, False]

    def hid_cols(k, c):
        at = 2 * pair_w + off[k] if both[k] else c * pair_w + off[k]
        return pl.ds(at if both[k] else pl.multiple_of(at, 128), width[k])

    def stats(k, c):
        cols, w = hid_cols(k, c), width[k]

        def body(i, _):
            rows = pl.ds(pl.multiple_of(i * 128, 128), 128)
            h = hid[rows, cols].astype(jnp.float32)
            hg_hi, hg_lo = hi_lo(h * gain_ref[cols][None, :])
            e = ein_cat[:, cols]
            code_acc[rows, :] += dot_nt(hg_hi, e) + dot_nt(hg_lo, e)
            sq = sq_acc[rows, :]
            for t in range(w // HD):
                ht = h[:, t * HD:(t + 1) * HD]
                sq = sq + ht * ht
            sq_acc[rows, :] = sq
            return 0

        leave(hid.at[:, cols], hid_out.at[:, cols])
        lax.fori_loop(0, tok // 128, body, 0)

    def act_mm(k):
        if not gained[0]:
            gained[0] = True
            for p in range(kvh):
                arrived(att.at[mine, att_cols(1 - f, p)], ar_sem.at[1, p])
        if both[k]:
            for dz in range(1 - nz, nz):
                for u, skip in ((r + 2 * dz, dz == 0), (2 * (zz + dz) + 1 - yy, False)):
                    if not skip:
                        when(inside(dz), lambda: arrived(wb[k].at[1 - g, u], xr_sem.at[k, u]))
        else:
            if not gained[1]:
                gained[1] = True
                for p in range(kvh):
                    arrived(att.at[other, att_cols(1 - f, p)], ar_sem.at[2, p])
            for dz in range(1 - nz, nz):
                if dz != 0:
                    act_cross(k, dz)
        wk = wb[k].reshape(2 * acols, width[k])

        def product(at):
            return jnp.dot(att[pl.ds(pl.multiple_of(at, QB), QB), :], wk[...], preferred_element_type=jnp.float32)

        if both[k]:
            def body(i, _):
                at = pl.multiple_of(i * QB, QB)
                hid[pl.ds(at, QB), hid_cols(k, g)] = product(at).astype(jnp.bfloat16)
                return 0

            lax.fori_loop(0, per, body, 0)
            stats(k, g)
        else:
            cols = slice(off[k], off[k] + width[k])

            def body(i, _):
                n = jnp.where(i < per, i, i - per)
                at = pl.multiple_of(n * QB, QB)
                d = product(jnp.where(i < per, tok, 0) + at).astype(jnp.bfloat16)

                @pl.when(i < per)
                def _():
                    hsend[pl.ds(at, QB), cols] = d

                def ends(j):
                    rows = pl.ds(j * QB, QB)
                    return hsend.at[rows, cols], hid.at[rows, hid_cols(k, g)], hr_sem.at[k, j]

                for j in range(per):
                    send(i == j, xnb, ends, j)
                    pending[-1] = (None, pending[-1][1])

                @pl.when(i >= per)
                def _():
                    hid[pl.ds(at, QB), hid_cols(k, g)] = d
                return 0

            lax.fori_loop(0, 2 * per, body, 0)
            stats(k, g)

    def act_hid(k):
        for j in range(per):
            arrived(hid.at[pl.ds(j * QB, QB), hid_cols(k, 1 - g)], hr_sem.at[k, j])
        stats(k, 1 - g)

    acts = {"own": act_own, "line": act_line, "cross": act_cross, "kvup": act_kvup, "kvy": act_kvy,
            "kvrelay": act_kvrelay, "tables": act_tables, "prep": act_prep, "rotk": act_rotk, "G": act_G,
            "att": act_att, "attfwd": act_attfwd, "mm": act_mm, "hid": act_hid}
    for name, *rest in ORDER if nz == 4 else plain_order(n_chunk, both, nz, kvh):
        acts[name](*rest)

    code = code_acc[...]
    code = code + pltpu.roll(code, HD // 2, 1)
    sq = jnp.sum(sq_acc[...], axis=1, keepdims=True)
    st_send[0:tok, :] = jnp.where(lane < HD // 2, code, sq)
    swap = pltpu.make_async_remote_copy(src_ref=st_send, dst_ref=st_recv, send_sem=st_sem.at[0], recv_sem=st_sem.at[1],
                                        device_id=part, device_id_type=MESH)
    swap.start()
    for cond, make in pending:
        when(cond, lambda make=make: make().wait_send())
    swap.wait()
    sums = st_send[0:tok, :] + st_recv[0:tok, :]
    turned_sums = pltpu.roll(sums, HD // 2, 1)
    code = jnp.where(lane < HD // 2, sums, turned_sums)
    total = jnp.where(lane < HD // 2, turned_sums, sums)
    inv_rms = lax.rsqrt(total * (1.0 / d_full) + norm_eps)
    mean_sum = st_send[tok:tok + 1, :] + st_recv[tok:tok + 1, :]
    c_hi, c_lo = hi_lo(inv_rms * code - mean_sum)
    c_ref[:, 0:HD] = c_hi
    c_ref[:, HD:2 * HD] = c_lo
    scale_ref[...] = inv_rms
    for c in left:
        c.wait()


def finish(c_hbm, scale_hbm, gain_hbm, hid_hbm, eout_hbm, out_hbm, c_ref, scale_ref, gain_ref, hid, eout, out, in_sem,
           out_sem):
    n = hid.shape[1] // TN

    def cols(i):
        return pl.ds(pl.multiple_of(i * TN, 128), TN)

    def come(i):
        return (pltpu.make_async_copy(eout_hbm.at[:, cols(i)], eout.at[:, cols(i)], in_sem.at[i]),
                pltpu.make_async_copy(hid_hbm.at[:, cols(i)], hid.at[:, cols(i)], in_sem.at[n + i]))

    def go(i):
        return pltpu.make_async_copy(out.at[:, cols(i)], out_hbm.at[:, cols(i)], out_sem.at[i])

    first = [pltpu.make_async_copy(src, dst, in_sem.at[2 * n + j]) for j, (src, dst) in enumerate(
        ((c_hbm, c_ref), (scale_hbm, scale_ref), (gain_hbm, gain_ref)))]
    for c in first:
        c.start()
    for i in range(n):
        for c in come(i):
            c.start()
    for c in first:
        c.wait()

    def body(i, _):
        for c in come(i):
            c.wait()
        e = eout[:, cols(i)]
        back = jnp.dot(c_ref[...], jnp.concatenate([e, e], axis=0), preferred_element_type=jnp.float32)
        h = hid[:, cols(i)].astype(jnp.float32) * jnp.concatenate([scale_ref[...]] * (TN // HD), axis=1)
        out[:, cols(i)] = (h * gain_ref[cols(i)][None, :] - back).astype(jnp.bfloat16)
        go(i).start()
        return 0

    lax.fori_loop(0, n, body, 0)
    for i in range(n):
        go(i).wait()


def solution(mesh):
    n_row = mesh.shape["row"]

    def on_device(queries, keys, values, out_proj, post_gain, mean_vec, erase_in, erase_out):
        tok = queries.shape[0]
        rows, d_full = out_proj.shape
        half = post_gain.shape[0]
        half_dim = HD // 2
        kvh = keys.shape[1] // HD
        inverse = np.exp(-(2.0 * np.arange(half_dim, dtype=np.float32) / HD) * np.log(np.float32(rope_base)))
        inverse = np.concatenate([inverse, inverse]).astype(np.float32)[None, :]
        any_spec = pl.BlockSpec(memory_space=pltpu.HBM)
        vm = pl.BlockSpec(memory_space=pltpu.VMEM)
        both, width, off, pair_w, both_w, via_z = plan(n_row)
        n_chunk = len(both)
        hops = n_row // 2 - 1
        n_ss = sum(6 + 4 * hops + b * (4 * hops + 1) + tok // QB for b in both) + 9 * kvh
        bf, f32 = jnp.bfloat16, jnp.float32
        dma = pltpu.SemaphoreType.DMA
        hidden, writing, code, scale = pl.pallas_call(
            functools.partial(kernel, n_row, d_full, n_ss),
            out_shape=[jax.ShapeDtypeStruct((tok, half), bf), jax.ShapeDtypeStruct((HD, half), bf),
                       jax.ShapeDtypeStruct((tok, 2 * HD), bf), jax.ShapeDtypeStruct((tok, HD), f32)],
            in_specs=[any_spec] * 9,
            out_specs=[pl.BlockSpec(memory_space=pl.ANY)] * 2 + [vm, vm],
            scratch_shapes=[pltpu.VMEM((2, n_row, rows, w), bf) for w in width] + [
                pltpu.VMEM(queries.shape, bf),
                pltpu.VMEM((kvh, 3 * tok, HD), bf),
                pltpu.VMEM((kvh, 3 * tok, HD), bf),
                pltpu.VMEM((kvh, 3 * tok, HD), bf),
                pltpu.VMEM((2 * tok, 2 * queries.shape[1]), bf),
                pltpu.VMEM((tok, half), bf),
                pltpu.VMEM((tok, pair_w), bf),
                pltpu.VMEM((3 * tok, HD), f32),
                pltpu.VMEM((3 * tok, HD), f32),
                pltpu.VMEM((HD, half), bf),
                pltpu.VMEM((HD, half), bf),
                pltpu.VMEM((tok, HD), f32),
                pltpu.VMEM((tok, HD), f32),
                pltpu.VMEM((tok + 8, HD), f32),
                pltpu.VMEM((tok + 8, HD), f32),
                pltpu.VMEM((half,), f32),
                pltpu.VMEM((half,), f32),
                pltpu.VMEM((erase_in.shape[1], half), f32),
                pltpu.VMEM((erase_in.shape[1], half), f32),
                pltpu.VMEM((1, HD), f32),
                dma((n_chunk + 2 * kvh + 6,)), dma((n_ss,)), dma((n_chunk, n_row)), dma((n_chunk, n_row)),
                dma((n_chunk,)), dma((2, kvh, 2)), dma((3, kvh)), dma((n_chunk, tok // QB)), dma((2,)),
                dma((1 + sum(1 if b else 2 for b in both),)),
            ],
            compiler_params=pltpu.CompilerParams(
                collective_id=0, has_side_effects=True, vmem_limit_bytes=60 * 1024 * 1024),
        )(queries, keys, values, out_proj, post_gain, mean_vec,
          erase_in.T, erase_out.T, jnp.asarray(inverse))
        return pl.pallas_call(
            finish,
            out_shape=jax.ShapeDtypeStruct((tok, half), bf),
            in_specs=[any_spec] * 5,
            out_specs=any_spec,
            scratch_shapes=[
                pltpu.VMEM((tok, 2 * HD), bf), pltpu.VMEM((tok, HD), f32), pltpu.VMEM((half,), f32),
                pltpu.VMEM((tok, half), bf), pltpu.VMEM((HD, half), bf), pltpu.VMEM((tok, half), bf),
                dma((2 * half // TN + 3,)), dma((half // TN,)),
            ],
            compiler_params=pltpu.CompilerParams(vmem_limit_bytes=60 * 1024 * 1024),
        )(code, scale, post_gain, hidden, writing)

    placed = (
        P(("grp", "row"), "col"),
        P(("grp", "row"), "col"),
        P(("grp", "row"), "col"),
        P(("col", "row"), None),
        P("col"),
        P("col"),
        P("col", None),
        P("col", None),
    )
    return jax.shard_map(
        on_device, mesh=mesh, in_specs=placed, out_specs=P(("grp", "row"), "col"), check_vma=False
    )
```

```python
import functools

import jax
import jax.numpy as jnp
import numpy as np
from jax import lax
from jax.experimental import pallas as pl
from jax.experimental.pallas import tpu as pltpu
from jax.sharding import PartitionSpec as P

HD = 128
WINDOW = 1024
MESH = pl.DeviceIdType.MESH
query_scale = 168.0 ** (-0.5)
norm_eps = 1e-06
rope_base = 10000.0
QB = 256
TN = 384
BIG = 1e30

CHUNKS = (("own", 128), ("pair", 512), ("pair", 384), ("pair", 256), ("pair", 128))
VIA_Z = (2, 3)
ORDER = (
    ("kvup", 2), ("kvup", 1), ("kvup", 0), ("own", 1), ("kvy", 1), ("kvup", 3), ("kvrelay", 2), ("line", 1, 1),
    ("kvy", 0), ("kvy", 2), ("kvy", 3), ("kvrelay", 1), ("tables",), ("prep",), ("kvrelay", 0), ("rotk", 1),
    ("cross", 1, 0), ("G", 1), ("att", 1), ("line", 1, -1), ("rotk", 2), ("G", 2), ("att", 2), ("rotk", 0),
    ("kvrelay", 3), ("own", 2), ("G", 0), ("line", 1, 2), ("att", 0), ("rotk", 3), ("line", 1, -2), ("attfwd", 1),
    ("line", 2, 1), ("G", 3), ("line", 2, -1), ("att", 3), ("line", 1, -3), ("line", 1, 3), ("attfwd", 2),
    ("line", 2, -2), ("line", 2, 2), ("attfwd", 0), ("own", 3), ("attfwd", 3), ("cross", 2, 0), ("mm", 1),
    ("line", 2, -3), ("line", 3, -1), ("line", 3, 1), ("line", 2, 3), ("own", 4), ("line", 3, 2), ("line", 3, -2),
    ("cross", 3, 0), ("mm", 2), ("line", 3, 3), ("line", 3, -3), ("line", 4, 1), ("line", 4, -1), ("own", 0),
    ("cross", 4, 0), ("line", 4, 2), ("line", 4, -2), ("mm", 3), ("line", 4, -3), ("line", 0, -1), ("line", 4, 3),
    ("line", 0, -2), ("line", 0, 1), ("cross", 0, 0), ("hid", 1), ("line", 0, 2), ("mm", 4), ("line", 0, -3),
    ("line", 0, 3), ("hid", 2), ("hid", 3), ("mm", 0), ("drain",), ("hid", 4),
)


def plain_order(kinds, nz, kvh):
    n_chunk = len(kinds)
    out = [("own", k) for k in range(n_chunk)]
    out += [(a, h) for h in range(kvh) for a in ("kvup", "kvy")]
    out += [("tables",), ("prep",)]
    out += [("kvrelay", h) for h in range(kvh)]
    for k in range(n_chunk):
        for d in range(1, nz):
            out += [("line", k, -d), ("line", k, d)]
        out += [("cross", k, 0)]
        if kinds[k] == "both":
            out += [("cross", k, d) for e in range(1, nz) for d in (-e, e)]
    for p in range(kvh):
        out += [("rotk", p), ("G", p), ("att", p)]
    out += [("attfwd", p) for p in range(kvh)]
    out += [("mm", k) for k in range(n_chunk)]
    out += [("hid", k) for k in range(n_chunk) if kinds[k] == "pair"]
    return out


def split_cat(x):
    hi = x.astype(jnp.bfloat16).astype(jnp.float32)
    return jnp.concatenate([hi, x - hi], axis=0).astype(jnp.bfloat16)


def hi_lo(x):
    hi = x.astype(jnp.bfloat16)
    return hi, (x - hi.astype(jnp.float32)).astype(jnp.bfloat16)


def dot_nt(x, y):
    return lax.dot_general(x, y, (((1,), (1,)), ((), ())), preferred_element_type=jnp.float32)


def plan(n_row):
    nz = n_row // 2
    chunks = CHUNKS if nz == 4 else (("both", 384), ("pair", 1152))
    via_z = VIA_Z if nz == 4 else (0,)
    kinds = [c[0] for c in chunks]
    width = [c[1] for c in chunks]
    off, pair_w, rest_w = [], 0, 0
    for kind, w in chunks:
        off.append(pair_w if kind == "pair" else rest_w)
        pair_w, rest_w = (pair_w + w, rest_w) if kind == "pair" else (pair_w, rest_w + w)
    return kinds, width, off, pair_w, rest_w, via_z


def kernel(n_row, d_full, n_ss, q_hbm, k_hbm, v_hbm, w_hbm, *rest):
    params_hbm, rest = rest[:5], rest[5:]
    hid_out, eout_out, c_ref, scale_ref, *scratch = rest
    kinds, width, off, pair_w, rest_w, via_z = plan(n_row)
    n_chunk = len(kinds)
    pair, both = [c == "pair" for c in kinds], [c == "both" for c in kinds]
    wb = scratch[:n_chunk]
    (qbuf, kbuf, vbuf, krot, att, hid, hsend, cosb, sinb, ein_cat, eout_cat, code_acc, sq_acc, st_send, st_recv,
     gain_ref, mean_ref, ein_ref, eout_ref, inv_ref, loc_sem, ss_sem, wr_sem, xr_sem, cr_sem, kr_sem, ar_sem, hr_sem, st_sem, out_sem) = scratch[n_chunk:]
    nz = n_row // 2
    g, r, f = lax.axis_index("grp"), lax.axis_index("row"), lax.axis_index("col")
    zz, yy = r // 2, r % 2
    has_up, has_dn = zz < nz - 1, zz > 0
    tok = qbuf.shape[0]
    half = pair_w * 2 + rest_w
    kvh = kbuf.shape[0]
    heads = qbuf.shape[1] // HD
    acols = heads * HD
    per = tok // QB

    part = {"grp": g, "row": r, "col": 1 - f}
    xnb = {"grp": 1 - g, "row": r, "col": f}
    ynb = {"grp": g, "row": 2 * zz + 1 - yy, "col": f}
    up = {"grp": g, "row": r + 2, "col": f}
    dn = {"grp": g, "row": r - 2, "col": f}

    barrier = pltpu.get_barrier_semaphore()
    for nb in (part, xnb, ynb):
        pl.semaphore_signal(barrier, inc=1, device_id=nb, device_id_type=MESH)

    @pl.when(has_up)
    def _():
        pl.semaphore_signal(barrier, inc=1, device_id=up, device_id_type=MESH)

    @pl.when(has_dn)
    def _():
        pl.semaphore_signal(barrier, inc=1, device_id=dn, device_id_type=MESH)

    def own_w(k, c):
        at = c * half + (g * pair_w + off[k] if pair[k] else 2 * pair_w + off[k])
        return w_hbm.at[:, pl.ds(pl.multiple_of(at, 128), width[k])]

    def head_cols(h):
        return pl.ds(h * HD, HD)

    own_rows = pl.ds(2 * tok, tok)
    loc_w = [pltpu.make_async_copy(own_w(k, f), wb[k].at[f, r], loc_sem.at[k]) for k in range(n_chunk)]
    loc_k = [pltpu.make_async_copy(k_hbm.at[:, head_cols(h)], kbuf.at[h, own_rows, :], loc_sem.at[n_chunk + h])
             for h in range(kvh)]
    loc_v = [pltpu.make_async_copy(v_hbm.at[:, head_cols(h)], vbuf.at[h, own_rows, :], loc_sem.at[n_chunk + kvh + h])
             for h in range(kvh)]
    loc_q = pltpu.make_async_copy(q_hbm, qbuf, loc_sem.at[n_chunk + 2 * kvh])
    loc_p = [pltpu.make_async_copy(src, dst, loc_sem.at[n_chunk + 2 * kvh + 1 + i]) for i, (src, dst) in enumerate(
        zip(params_hbm, (gain_ref, mean_ref, ein_ref, eout_ref, inv_ref)))]
    for c in loc_w + loc_k + loc_v + [loc_q] + loc_p:
        c.start()

    pl.semaphore_wait(barrier, 3 + has_up.astype(jnp.int32) + has_dn.astype(jnp.int32))

    pending = []
    left = []

    def leave(src, dst):
        c = pltpu.make_async_copy(src, dst, out_sem.at[len(left)])
        left.append(c)
        c.start()

    def send(cond, dev, ends, *args):
        i = len(pending)
        assert i < n_ss, i

        def make():
            src, dst, recv = ends(*args)
            return pltpu.make_async_remote_copy(
                src_ref=src, dst_ref=dst, send_sem=ss_sem.at[i], recv_sem=recv, device_id=dev, device_id_type=MESH)

        pending.append((cond, make))
        if cond is None:
            make().start()
        else:
            @pl.when(cond)
            def _():
                make().start()

    def when(cond, fn):
        if cond is None:
            fn()
        else:
            pl.when(cond)(fn)

    def arrived(ref, sem):
        pltpu.make_async_copy(ref, ref, sem).wait()

    for k in range(n_chunk):
        send(None, part, lambda k: (own_w(k, 1 - f), wb[k].at[f, r], cr_sem.at[k]), k)

    def block(k, u):
        return wb[k].at[g, u] if both[k] else wb[k].at[:, u]

    def send_w(cond, k, u, dev):
        send(cond, dev, lambda: (block(k, u), block(k, u), wr_sem.at[k, u]))

    def send_x(cond, k, u):
        send(cond, xnb, lambda: (wb[k].at[g, u], wb[k].at[g, u], xr_sem.at[k, u]))

    def act_own(k):
        loc_w[k].wait()
        arrived(wb[k].at[1 - f, r], cr_sem.at[k])
        send_w(has_up, k, r, up)
        send_w(has_dn, k, r, dn)
        send_w(None, k, r, ynb)

    def inside(dz):
        return None if dz == 0 else (zz + dz >= 0 if dz < 0 else zz + dz < nz)

    def act_line(k, dz):
        cond, u = inside(dz), r + 2 * dz
        when(cond, lambda: arrived(block(k, u), wr_sem.at[k, u]))
        if dz < 0:
            send_w(cond & has_up, k, u, up)
        else:
            send_w(cond & has_dn, k, u, dn)
        if dz != 1:
            send_w(cond & has_up if dz == -1 and k in via_z else cond, k, u, ynb)
        if both[k]:
            send_x(cond, k, u)

    def act_cross(k, dz):
        cond, u = inside(dz), 2 * (zz + dz) + 1 - yy
        when(cond, lambda: arrived(block(k, u), wr_sem.at[k, u]))
        if dz == 0:
            send_w(has_dn, k, u, dn)
            if k in via_z:
                send_w(zz == nz - 2, k, u, up)
        if both[k]:
            send_x(cond, k, u)

    def kv_rows(slot):
        return pl.ds(slot * tok, tok)

    def send_kv(cond, h, src_slot, slot, dev):
        def ends(n):
            hbm, buf = ((k_hbm, kbuf), (v_hbm, vbuf))[n]
            src = hbm.at[:, head_cols(h)] if src_slot == 2 else buf.at[h, kv_rows(src_slot), :]
            return src, buf.at[h, kv_rows(slot), :], kr_sem.at[slot, h, n]

        for n in range(2):
            send(cond, dev, ends, n)

    def wait_kv(cond, h, slot):
        @pl.when(cond)
        def _():
            for n, buf in enumerate((kbuf, vbuf)):
                arrived(buf.at[h, kv_rows(slot), :], kr_sem.at[slot, h, n])

    def act_kvup(h):
        send_kv(has_up, h, 2, 0, up)

    def act_kvy(h):
        send_kv(yy == 0, h, 2, 1, ynb)

    def act_kvrelay(h):
        wait_kv(has_dn, h, 0)
        send_kv(has_dn & (yy == 1), h, 0, 1, ynb)

    sign = jnp.where(lax.broadcasted_iota(jnp.int32, (1, HD), 1) < HD // 2, -1.0, 1.0)
    key_base = r * tok - 2 * tok

    def table(i, _):
        at = pl.multiple_of(i * 128, 128)
        pos = (key_base + at + lax.broadcasted_iota(jnp.int32, (128, HD), 0)).astype(jnp.float32)
        ang = pos * inv_ref[...]
        cosb[pl.ds(at, 128), :] = jnp.cos(ang)
        sinb[pl.ds(at, 128), :] = jnp.sin(ang) * sign
        return 0

    def turned(x, at):
        x = x.astype(jnp.float32)
        cs, sn = cosb[pl.ds(at, 128), :], sinb[pl.ds(at, 128), :]
        return (x * cs + pltpu.roll(x, HD // 2, 1) * sn).astype(jnp.bfloat16)

    def rot_q(i, _):
        at = pl.multiple_of(i * 128, 128)
        for h in range(heads):
            cols = slice(h * HD, (h + 1) * HD)
            qbuf[pl.ds(at, 128), cols] = turned(qbuf[pl.ds(at, 128), cols], 2 * tok + at)
        return 0

    def rot_own(i, _):
        at = pl.multiple_of(2 * tok + i * 128, 128)
        for h in range(kvh):
            krot[h, pl.ds(at, 128), :] = turned(kbuf[h, pl.ds(at, 128), :], at)
        return 0

    def act_tables():
        @pl.when(zz == 0)
        def _():
            kbuf[:, kv_rows(0), :] = jnp.zeros((kvh, tok, HD), kbuf.dtype)
            vbuf[:, kv_rows(0), :] = jnp.zeros((kvh, tok, HD), vbuf.dtype)

        @pl.when(r == 0)
        def _():
            kbuf[:, kv_rows(1), :] = jnp.zeros((kvh, tok, HD), kbuf.dtype)
            vbuf[:, kv_rows(1), :] = jnp.zeros((kvh, tok, HD), vbuf.dtype)

        for c in loc_p:
            c.wait()
        lax.fori_loop(0, 3 * tok // 128, table, 0)

    def prep(i, m_acc):
        cols = pl.ds(pl.multiple_of(i * 384, 128), 384)
        e = ein_ref[:, cols]
        ein_cat[:, cols] = split_cat(e * gain_ref[cols][None, :])
        e = split_cat(e)
        m_hi, m_lo = hi_lo(jnp.broadcast_to(mean_ref[cols][None, :], (16, 384)))
        m_acc = m_acc + dot_nt(m_hi, e) + dot_nt(m_lo, e)
        eout_cat[:, cols] = split_cat(eout_ref[:, cols])
        return m_acc

    def act_prep():
        loc_q.wait()
        lax.fori_loop(0, tok // 128, rot_q, 0)
        for c in loc_k + loc_v:
            c.wait()
        lax.fori_loop(0, tok // 128, rot_own, 0)
        m_acc = lax.fori_loop(0, half // 384, prep, jnp.zeros((16, HD), jnp.float32))
        leave(eout_cat, eout_out)
        st_send[tok:tok + 8, :] = (m_acc + pltpu.roll(m_acc, HD // 2, 1))[0:8]
        code_acc[...] = jnp.zeros_like(code_acc)
        sq_acc[...] = jnp.zeros_like(sq_acc)

    def act_rotk(h):
        wait_kv(r > 0, h, 1)

        def body(i, _):
            at = pl.multiple_of(i * 128, 128)
            krot[h, pl.ds(at, 128), :] = turned(kbuf[h, pl.ds(at, 128), :], at)
            return 0

        lax.fori_loop(0, 2 * tok // 128, body, 0)

    nt = WINDOW // QB + 1
    ri = lax.broadcasted_iota(jnp.int32, (QB, QB), 0)
    ci = lax.broadcasted_iota(jnp.int32, (QB, QB), 1)
    pen = [jnp.where(zz > 0, 0.0, BIG), jnp.where(r > 0, 0.0, BIG), jnp.float32(0.0)]

    def act_G(kv):
        def piece(j, _):
            head, i = (heads // kvh) * kv + j // per, j % per
            rows = pl.ds(pl.multiple_of(i * QB, QB), QB)
            qt = qbuf[rows, pl.ds(pl.multiple_of(head * HD, HD), HD)]
            key_rows = pl.ds(pl.multiple_of(i * QB, QB), nt * QB)
            s = dot_nt(qt, krot[kv, key_rows, :]) * query_scale
            tiles, bias, m = [], [], None
            for t in range(nt):
                st = s[:, t * QB:(t + 1) * QB]
                if t == 0:
                    st = jnp.where(ci > ri, st, -BIG)
                if t == nt - 1:
                    st = jnp.where(ci <= ri, st, -BIG)
                blk = (i + t) // per
                b = jnp.where(blk == 0, pen[0], jnp.where(blk == 1, pen[1], pen[2]))
                mt = jnp.max(st, axis=1, keepdims=True) - b
                m = mt if m is None else jnp.maximum(m, mt)
                tiles.append(st)
                bias.append(b)
            es, tot = [], None
            for st, b in zip(tiles, bias):
                e = jnp.exp(st - (m + b))
                es.append(e)
                se = jnp.sum(e, axis=1, keepdims=True)
                tot = se if tot is None else tot + se
            inv = 1.0 / tot
            p = jnp.concatenate([(e * inv).astype(jnp.bfloat16) for e in es], axis=1)
            o = jnp.dot(p, vbuf[kv, key_rows, :], preferred_element_type=jnp.float32)
            att[rows, pl.ds(pl.multiple_of(f * acols + head * HD, HD), HD)] = o.astype(jnp.bfloat16)
            return 0

        lax.fori_loop(0, (heads // kvh) * per, piece, 0)

    group = heads // kvh * HD
    mine, other = pl.ds(0, tok), pl.ds(tok, tok)

    def att_cols(c, p):
        return pl.ds(pl.multiple_of(c * acols + p * group, 128), group)

    def act_att(p):
        cols = att_cols(f, p)
        send(None, xnb, lambda: (att.at[mine, cols], att.at[other, cols], ar_sem.at[0, p]))
        send(None, part, lambda: (att.at[mine, cols], att.at[mine, cols], ar_sem.at[1, p]))

    def act_attfwd(p):
        cols = att_cols(f, p)
        arrived(att.at[other, cols], ar_sem.at[0, p])
        send(None, part, lambda: (att.at[other, cols], att.at[other, cols], ar_sem.at[2, p]))

    lane = lax.broadcasted_iota(jnp.int32, (tok, HD), 1)
    gained = [False, False]
    mark, drained = [0], [0]

    def hid_cols(k, c):
        return pl.ds(pl.multiple_of(c * pair_w + off[k], 128) if pair[k] else 2 * pair_w + off[k], width[k])

    def stats(k, c):
        cols, w = hid_cols(k, c), width[k]

        def body(i, _):
            rows = pl.ds(pl.multiple_of(i * QB, QB), QB)
            h = hid[rows, cols]
            code_acc[rows, :] += dot_nt(h, ein_cat[:, cols])
            h = h.astype(jnp.float32)
            sq = sq_acc[rows, :]
            for t in range(w // HD):
                ht = h[:, t * HD:(t + 1) * HD]
                sq = sq + ht * ht
            sq_acc[rows, :] = sq
            return 0

        leave(hid.at[:, cols], hid_out.at[:, cols])
        lax.fori_loop(0, per, body, 0)

    def act_mm(k):
        mark[0] = len(pending)
        if not gained[0]:
            gained[0] = True
            for p in range(kvh):
                arrived(att.at[mine, att_cols(1 - f, p)], ar_sem.at[1, p])
        if pair[k] and not gained[1]:
            gained[1] = True
            for p in range(kvh):
                arrived(att.at[other, att_cols(1 - f, p)], ar_sem.at[2, p])
        if both[k]:
            for dz in range(1 - nz, nz):
                for u, skip in ((r + 2 * dz, dz == 0), (2 * (zz + dz) + 1 - yy, False)):
                    if not skip:
                        when(inside(dz), lambda: arrived(wb[k].at[1 - g, u], xr_sem.at[k, u]))
        else:
            for dz in range(1 - nz, nz):
                if dz != 0:
                    act_cross(k, dz)
        wk = wb[k].reshape(2 * acols, width[k])

        def product(at):
            return jnp.dot(att[pl.ds(pl.multiple_of(at, QB), QB), :], wk[...], preferred_element_type=jnp.float32)

        if not pair[k]:
            def body(i, _):
                at = pl.multiple_of(i * QB, QB)
                hid[pl.ds(at, QB), hid_cols(k, g)] = product(at).astype(jnp.bfloat16)
                return 0

            lax.fori_loop(0, per, body, 0)
            stats(k, g)
        else:
            cols = slice(off[k], off[k] + width[k])

            def body(i, _):
                n = jnp.where(i < per, i, i - per)
                at = pl.multiple_of(n * QB, QB)
                d = product(jnp.where(i < per, tok, 0) + at).astype(jnp.bfloat16)

                @pl.when(i < per)
                def _():
                    hsend[pl.ds(at, QB), cols] = d

                def ends(j):
                    rows = pl.ds(j * QB, QB)
                    return hsend.at[rows, cols], hid.at[rows, hid_cols(k, g)], hr_sem.at[k, j]

                for j in range(per):
                    send(i == j, xnb, ends, j)
                    pending[-1] = (None, pending[-1][1])

                @pl.when(i >= per)
                def _():
                    hid[pl.ds(at, QB), hid_cols(k, g)] = d
                return 0

            lax.fori_loop(0, 2 * per, body, 0)
            stats(k, g)

    def act_hid(k):
        for j in range(per):
            arrived(hid.at[pl.ds(j * QB, QB), hid_cols(k, 1 - g)], hr_sem.at[k, j])
        stats(k, 1 - g)

    def drain(end):
        for cond, make in pending[drained[0]:end]:
            when(cond, lambda make=make: make().wait_send())
        drained[0] = end

    def act_drain():
        drain(mark[0])

    acts = {"drain": act_drain, "own": act_own, "line": act_line, "cross": act_cross, "kvup": act_kvup, "kvy": act_kvy,
            "kvrelay": act_kvrelay, "tables": act_tables, "prep": act_prep, "rotk": act_rotk, "G": act_G,
            "att": act_att, "attfwd": act_attfwd, "mm": act_mm, "hid": act_hid}
    for name, *rest in ORDER if nz == 4 else plain_order(kinds, nz, kvh):
        acts[name](*rest)

    code = code_acc[...]
    code = code + pltpu.roll(code, HD // 2, 1)
    sq = jnp.sum(sq_acc[...], axis=1, keepdims=True)
    st_send[0:tok, :] = jnp.where(lane < HD // 2, code, sq)
    swap = pltpu.make_async_remote_copy(src_ref=st_send, dst_ref=st_recv, send_sem=st_sem.at[0], recv_sem=st_sem.at[1],
                                        device_id=part, device_id_type=MESH)
    swap.start()
    drain(len(pending))
    swap.wait()
    sums = st_send[0:tok, :] + st_recv[0:tok, :]
    turned_sums = pltpu.roll(sums, HD // 2, 1)
    code = jnp.where(lane < HD // 2, sums, turned_sums)
    total = jnp.where(lane < HD // 2, turned_sums, sums)
    inv_rms = lax.rsqrt(total * (1.0 / d_full) + norm_eps)
    mean_sum = st_send[tok:tok + 1, :] + st_recv[tok:tok + 1, :]
    c_hi, c_lo = hi_lo(inv_rms * code - mean_sum)
    c_ref[:, 0:HD] = c_hi
    c_ref[:, HD:2 * HD] = c_lo
    scale_ref[...] = inv_rms
    for c in left:
        c.wait()


def finish(c_hbm, scale_hbm, gain_hbm, hid_hbm, eout_hbm, out_hbm, c_ref, scale_ref, gain_ref, hid, eout, out, in_sem,
           out_sem):
    n = hid.shape[1] // TN

    def cols(i):
        return pl.ds(pl.multiple_of(i * TN, 128), TN)

    def come(i):
        return (pltpu.make_async_copy(eout_hbm.at[:, cols(i)], eout.at[:, cols(i)], in_sem.at[i]),
                pltpu.make_async_copy(hid_hbm.at[:, cols(i)], hid.at[:, cols(i)], in_sem.at[n + i]))

    def go(i):
        return pltpu.make_async_copy(out.at[:, cols(i)], out_hbm.at[:, cols(i)], out_sem.at[i])

    first = [pltpu.make_async_copy(src, dst, in_sem.at[2 * n + j]) for j, (src, dst) in enumerate(
        ((c_hbm, c_ref), (scale_hbm, scale_ref), (gain_hbm, gain_ref)))]
    for c in first:
        c.start()
    for i in range(n):
        for c in come(i):
            c.start()
    for c in first:
        c.wait()

    def body(i, _):
        for c in come(i):
            c.wait()
        e = eout[:, cols(i)]
        back = jnp.dot(c_ref[...], jnp.concatenate([e, e], axis=0), preferred_element_type=jnp.float32)
        h = hid[:, cols(i)].astype(jnp.float32) * jnp.concatenate([scale_ref[...]] * (TN // HD), axis=1)
        out[:, cols(i)] = (h * gain_ref[cols(i)][None, :] - back).astype(jnp.bfloat16)
        go(i).start()
        return 0

    lax.fori_loop(0, n, body, 0)
    for i in range(n):
        go(i).wait()


def solution(mesh):
    n_row = mesh.shape["row"]

    def on_device(queries, keys, values, out_proj, post_gain, mean_vec, erase_in, erase_out):
        tok = queries.shape[0]
        rows, d_full = out_proj.shape
        half = post_gain.shape[0]
        half_dim = HD // 2
        kvh = keys.shape[1] // HD
        inverse = np.exp(-(2.0 * np.arange(half_dim, dtype=np.float32) / HD) * np.log(np.float32(rope_base)))
        inverse = np.concatenate([inverse, inverse]).astype(np.float32)[None, :]
        any_spec = pl.BlockSpec(memory_space=pltpu.HBM)
        vm = pl.BlockSpec(memory_space=pltpu.VMEM)
        kinds, width, off, pair_w, rest_w, via_z = plan(n_row)
        n_chunk = len(kinds)
        hops = n_row // 2 - 1
        n_ss = sum(6 + 4 * hops + (b == "both") * (4 * hops + 1) + tok // QB for b in kinds) + 9 * kvh
        bf, f32 = jnp.bfloat16, jnp.float32
        dma = pltpu.SemaphoreType.DMA
        hidden, writing, code, scale = pl.pallas_call(
            functools.partial(kernel, n_row, d_full, n_ss),
            out_shape=[jax.ShapeDtypeStruct((tok, half), bf), jax.ShapeDtypeStruct((HD, half), bf),
                       jax.ShapeDtypeStruct((tok, 2 * HD), bf), jax.ShapeDtypeStruct((tok, HD), f32)],
            in_specs=[any_spec] * 9,
            out_specs=[pl.BlockSpec(memory_space=pl.ANY)] * 2 + [vm, vm],
            scratch_shapes=[pltpu.VMEM((2, n_row, rows, w), bf) for w in width] + [
                pltpu.VMEM(queries.shape, bf),
                pltpu.VMEM((kvh, 3 * tok, HD), bf),
                pltpu.VMEM((kvh, 3 * tok, HD), bf),
                pltpu.VMEM((kvh, 3 * tok, HD), bf),
                pltpu.VMEM((2 * tok, 2 * queries.shape[1]), bf),
                pltpu.VMEM((tok, half), bf),
                pltpu.VMEM((tok, pair_w), bf),
                pltpu.VMEM((3 * tok, HD), f32),
                pltpu.VMEM((3 * tok, HD), f32),
                pltpu.VMEM((HD, half), bf),
                pltpu.VMEM((HD, half), bf),
                pltpu.VMEM((tok, HD), f32),
                pltpu.VMEM((tok, HD), f32),
                pltpu.VMEM((tok + 8, HD), f32),
                pltpu.VMEM((tok + 8, HD), f32),
                pltpu.VMEM((half,), f32),
                pltpu.VMEM((half,), f32),
                pltpu.VMEM((erase_in.shape[1], half), f32),
                pltpu.VMEM((erase_in.shape[1], half), f32),
                pltpu.VMEM((1, HD), f32),
                dma((n_chunk + 2 * kvh + 6,)), dma((n_ss,)), dma((n_chunk, n_row)), dma((n_chunk, n_row)),
                dma((n_chunk,)), dma((2, kvh, 2)), dma((3, kvh)), dma((n_chunk, tok // QB)), dma((2,)),
                dma((1 + sum(2 if b == "pair" else 1 for b in kinds),)),
            ],
            compiler_params=pltpu.CompilerParams(
                collective_id=0, has_side_effects=True, vmem_limit_bytes=60 * 1024 * 1024),
        )(queries, keys, values, out_proj, post_gain, mean_vec,
          erase_in.T, erase_out.T, jnp.asarray(inverse))
        return pl.pallas_call(
            finish,
            out_shape=jax.ShapeDtypeStruct((tok, half), bf),
            in_specs=[any_spec] * 5,
            out_specs=any_spec,
            scratch_shapes=[
                pltpu.VMEM((tok, 2 * HD), bf), pltpu.VMEM((tok, HD), f32), pltpu.VMEM((half,), f32),
                pltpu.VMEM((tok, half), bf), pltpu.VMEM((HD, half), bf), pltpu.VMEM((tok, half), bf),
                dma((2 * half // TN + 3,)), dma((half // TN,)),
            ],
            compiler_params=pltpu.CompilerParams(vmem_limit_bytes=60 * 1024 * 1024),
        )(code, scale, post_gain, hidden, writing)

    placed = (
        P(("grp", "row"), "col"),
        P(("grp", "row"), "col"),
        P(("grp", "row"), "col"),
        P(("col", "row"), None),
        P("col"),
        P("col"),
        P("col", None),
        P("col", None),
    )
    return jax.shard_map(
        on_device, mesh=mesh, in_specs=placed, out_specs=P(("grp", "row"), "col"), check_vma=False
    )
```

```python
import functools

import jax
import jax.numpy as jnp
import numpy as np
from jax import lax
from jax.experimental import pallas as pl
from jax.experimental.pallas import tpu as pltpu
from jax.sharding import PartitionSpec as P

HD = 128
WINDOW = 1024
MESH = pl.DeviceIdType.MESH
query_scale = 168.0 ** (-0.5)
norm_eps = 1e-06
rope_base = 10000.0
QB = 256
TN = 896
BIG = 1e30

CHUNKS = (("own", 128), ("pair", 512), ("pair", 256), ("pair", 256), ("pair", 256))
VIA_Z = (2, 3)
ORDER = (
    ("kvup", 3), ("kvup", 1), ("kvy", 3), ("kvup", 2), ("kvup", 0), ("own", 1), ("tables",), ("kvy", 1), ("own", 4),
    ("kvrelay", 3), ("kvy", 2), ("prep",), ("line", 4, 1), ("kvrelay", 1), ("cross", 1, 0), ("rotk", 3), ("kvy", 0),
    ("G", 3), ("kvrelay", 2), ("line", 1, 1), ("att", 3), ("rotk", 1), ("G", 1), ("att", 1), ("kvrelay", 0),
    ("rotk", 2), ("line", 1, 2), ("line", 1, -1), ("G", 2), ("att", 2), ("rotk", 0), ("own", 3), ("cross", 4, 0),
    ("G", 0), ("line", 1, -2), ("att", 0), ("attfwd", 3), ("own", 0), ("line", 1, -3), ("attfwd", 1), ("line", 1, 3),
    ("attfwd", 2), ("line", 4, -1), ("line", 3, 1), ("own", 2), ("attfwd", 0), ("line", 4, 2), ("line", 4, -2),
    ("line", 0, 1), ("line", 3, -1), ("mm", 1), ("line", 2, -1), ("line", 2, 1), ("line", 4, 3), ("line", 4, -3),
    ("line", 3, -2), ("line", 3, 2), ("cross", 3, 0), ("line", 2, 2), ("cross", 0, 0), ("line", 3, -3),
    ("line", 2, -2), ("line", 3, 3), ("cross", 2, 0), ("mm", 4), ("line", 0, 2), ("line", 2, -3), ("line", 2, 3),
    ("line", 0, -1), ("mm", 3), ("mm", 2), ("line", 0, 3), ("line", 0, -3), ("line", 0, -2), ("hid", 1), ("hid", 4),
    ("hid", 3), ("mm", 0), ("drain",), ("hid", 2),
)


def plain_order(kinds, nz, kvh):
    n_chunk = len(kinds)
    out = [("own", k) for k in range(n_chunk)]
    out += [(a, h) for h in range(kvh) for a in ("kvup", "kvy")]
    out += [("tables",), ("prep",)]
    out += [("kvrelay", h) for h in range(kvh)]
    for k in range(n_chunk):
        for d in range(1, nz):
            out += [("line", k, -d), ("line", k, d)]
        out += [("cross", k, 0)]
        if kinds[k] == "both":
            out += [("cross", k, d) for e in range(1, nz) for d in (-e, e)]
    for p in range(kvh):
        out += [("rotk", p), ("G", p), ("att", p)]
    out += [("attfwd", p) for p in range(kvh)]
    out += [("mm", k) for k in range(n_chunk)]
    out += [("hid", k) for k in range(n_chunk) if kinds[k] == "pair"]
    return out


def split_cat(x):
    hi = x.astype(jnp.bfloat16).astype(jnp.float32)
    return jnp.concatenate([hi, x - hi], axis=0).astype(jnp.bfloat16)


def hi_lo(x):
    hi = x.astype(jnp.bfloat16)
    return hi, (x - hi.astype(jnp.float32)).astype(jnp.bfloat16)


def dot_nt(x, y):
    return lax.dot_general(x, y, (((1,), (1,)), ((), ())), preferred_element_type=jnp.float32)


def plan(n_row):
    nz = n_row // 2
    chunks = CHUNKS if nz == 4 else (("both", 384), ("pair", 1152))
    via_z = VIA_Z if nz == 4 else (0,)
    kinds = [c[0] for c in chunks]
    width = [c[1] for c in chunks]
    off, pair_w, rest_w = [], 0, 0
    for kind, w in chunks:
        off.append(pair_w if kind == "pair" else rest_w)
        pair_w, rest_w = (pair_w + w, rest_w) if kind == "pair" else (pair_w, rest_w + w)
    return kinds, width, off, pair_w, rest_w, via_z


def kernel(n_row, d_full, n_ss, q_hbm, k_hbm, v_hbm, w_hbm, *rest):
    params_hbm, rest = rest[:5], rest[5:]
    hid_out, eout_out, c_ref, scale_ref, *scratch = rest
    kinds, width, off, pair_w, rest_w, via_z = plan(n_row)
    n_chunk = len(kinds)
    pair, both = [c == "pair" for c in kinds], [c == "both" for c in kinds]
    wb = scratch[:n_chunk]
    (qbuf, kbuf, vbuf, krot, att, hid, hsend, cosb, sinb, ein_cat, eout_cat, code_acc, sq_acc, st_send, st_recv,
     gain_ref, mean_ref, ein_ref, eout_ref, inv_ref, loc_sem, ss_sem, wr_sem, xr_sem, cr_sem, kr_sem, ar_sem, hr_sem, st_sem, out_sem) = scratch[n_chunk:]
    nz = n_row // 2
    g, r, f = lax.axis_index("grp"), lax.axis_index("row"), lax.axis_index("col")
    zz, yy = r // 2, r % 2
    has_up, has_dn = zz < nz - 1, zz > 0
    tok = qbuf.shape[0]
    half = pair_w * 2 + rest_w
    kvh = kbuf.shape[0]
    heads = qbuf.shape[1] // HD
    acols = heads * HD
    per = tok // QB

    part = {"grp": g, "row": r, "col": 1 - f}
    xnb = {"grp": 1 - g, "row": r, "col": f}
    ynb = {"grp": g, "row": 2 * zz + 1 - yy, "col": f}
    up = {"grp": g, "row": r + 2, "col": f}
    dn = {"grp": g, "row": r - 2, "col": f}

    barrier = pltpu.get_barrier_semaphore()
    for nb in (part, xnb, ynb):
        pl.semaphore_signal(barrier, inc=1, device_id=nb, device_id_type=MESH)

    @pl.when(has_up)
    def _():
        pl.semaphore_signal(barrier, inc=1, device_id=up, device_id_type=MESH)

    @pl.when(has_dn)
    def _():
        pl.semaphore_signal(barrier, inc=1, device_id=dn, device_id_type=MESH)

    def own_w(k, c):
        at = c * half + (g * pair_w + off[k] if pair[k] else 2 * pair_w + off[k])
        return w_hbm.at[:, pl.ds(pl.multiple_of(at, 128), width[k])]

    def head_cols(h):
        return pl.ds(h * HD, HD)

    own_rows = pl.ds(2 * tok, tok)
    loc_w = [pltpu.make_async_copy(own_w(k, f), wb[k].at[f, r], loc_sem.at[k]) for k in range(n_chunk)]
    loc_k = [pltpu.make_async_copy(k_hbm.at[:, head_cols(h)], kbuf.at[h, own_rows, :], loc_sem.at[n_chunk + h])
             for h in range(kvh)]
    loc_v = [pltpu.make_async_copy(v_hbm.at[:, head_cols(h)], vbuf.at[h, own_rows, :], loc_sem.at[n_chunk + kvh + h])
             for h in range(kvh)]
    loc_q = pltpu.make_async_copy(q_hbm, qbuf, loc_sem.at[n_chunk + 2 * kvh])
    loc_p = [pltpu.make_async_copy(src, dst, loc_sem.at[n_chunk + 2 * kvh + 1 + i]) for i, (src, dst) in enumerate(
        zip(params_hbm, (gain_ref, mean_ref, ein_ref, eout_ref, inv_ref)))]
    for c in loc_w + loc_k + loc_v + [loc_q] + loc_p:
        c.start()

    pl.semaphore_wait(barrier, 3 + has_up.astype(jnp.int32) + has_dn.astype(jnp.int32))

    pending = []
    left = []

    def leave(src, dst):
        c = pltpu.make_async_copy(src, dst, out_sem.at[len(left)])
        left.append(c)
        c.start()

    def send(cond, dev, ends, *args):
        i = len(pending)
        assert i < n_ss, i

        def make():
            src, dst, recv = ends(*args)
            return pltpu.make_async_remote_copy(
                src_ref=src, dst_ref=dst, send_sem=ss_sem.at[i], recv_sem=recv, device_id=dev, device_id_type=MESH)

        pending.append((cond, make))
        if cond is None:
            make().start()
        else:
            @pl.when(cond)
            def _():
                make().start()

    def when(cond, fn):
        if cond is None:
            fn()
        else:
            pl.when(cond)(fn)

    def arrived(ref, sem):
        pltpu.make_async_copy(ref, ref, sem).wait()

    for k in range(n_chunk):
        send(None, part, lambda k: (own_w(k, 1 - f), wb[k].at[f, r], cr_sem.at[k]), k)

    def block(k, u):
        return wb[k].at[g, u] if both[k] else wb[k].at[:, u]

    def send_w(cond, k, u, dev):
        send(cond, dev, lambda: (block(k, u), block(k, u), wr_sem.at[k, u]))

    def send_x(cond, k, u):
        send(cond, xnb, lambda: (wb[k].at[g, u], wb[k].at[g, u], xr_sem.at[k, u]))

    def act_own(k):
        loc_w[k].wait()
        arrived(wb[k].at[1 - f, r], cr_sem.at[k])
        send_w(has_up, k, r, up)
        send_w(has_dn, k, r, dn)
        send_w(None, k, r, ynb)

    def inside(dz):
        return None if dz == 0 else (zz + dz >= 0 if dz < 0 else zz + dz < nz)

    def act_line(k, dz):
        cond, u = inside(dz), r + 2 * dz
        when(cond, lambda: arrived(block(k, u), wr_sem.at[k, u]))
        if dz < 0:
            send_w(cond & has_up, k, u, up)
        else:
            send_w(cond & has_dn, k, u, dn)
        if dz != 1:
            send_w(cond & has_up if dz == -1 and k in via_z else cond, k, u, ynb)
        if both[k]:
            send_x(cond, k, u)

    def act_cross(k, dz):
        cond, u = inside(dz), 2 * (zz + dz) + 1 - yy
        when(cond, lambda: arrived(block(k, u), wr_sem.at[k, u]))
        if dz == 0:
            send_w(has_dn, k, u, dn)
            if k in via_z:
                send_w(zz == nz - 2, k, u, up)
        if both[k]:
            send_x(cond, k, u)

    def kv_rows(slot):
        return pl.ds(slot * tok, tok)

    def send_kv(cond, h, src_slot, slot, dev):
        def ends(n):
            hbm, buf = ((k_hbm, kbuf), (v_hbm, vbuf))[n]
            src = hbm.at[:, head_cols(h)] if src_slot == 2 else buf.at[h, kv_rows(src_slot), :]
            return src, buf.at[h, kv_rows(slot), :], kr_sem.at[slot, h, n]

        for n in range(2):
            send(cond, dev, ends, n)

    def wait_kv(cond, h, slot):
        @pl.when(cond)
        def _():
            for n, buf in enumerate((kbuf, vbuf)):
                arrived(buf.at[h, kv_rows(slot), :], kr_sem.at[slot, h, n])

    def act_kvup(h):
        send_kv(has_up, h, 2, 0, up)

    def act_kvy(h):
        send_kv(yy == 0, h, 2, 1, ynb)

    def act_kvrelay(h):
        wait_kv(has_dn, h, 0)
        send_kv(has_dn & (yy == 1), h, 0, 1, ynb)

    sign = jnp.where(lax.broadcasted_iota(jnp.int32, (1, HD), 1) < HD // 2, -1.0, 1.0)
    key_base = r * tok - 2 * tok

    def table(i, _):
        at = pl.multiple_of(i * 128, 128)
        pos = (key_base + at + lax.broadcasted_iota(jnp.int32, (128, HD), 0)).astype(jnp.float32)
        ang = pos * inv_ref[...]
        cosb[pl.ds(at, 128), :] = jnp.cos(ang)
        sinb[pl.ds(at, 128), :] = jnp.sin(ang) * sign
        return 0

    def turned(x, at):
        x = x.astype(jnp.float32)
        cs, sn = cosb[pl.ds(at, 128), :], sinb[pl.ds(at, 128), :]
        return (x * cs + pltpu.roll(x, HD // 2, 1) * sn).astype(jnp.bfloat16)

    def rot_q(i, _):
        at = pl.multiple_of(i * 128, 128)
        for h in range(heads):
            cols = slice(h * HD, (h + 1) * HD)
            qbuf[pl.ds(at, 128), cols] = turned(qbuf[pl.ds(at, 128), cols], 2 * tok + at)
        return 0

    def rot_own(i, _):
        at = pl.multiple_of(2 * tok + i * 128, 128)
        for h in range(kvh):
            krot[h, pl.ds(at, 128), :] = turned(kbuf[h, pl.ds(at, 128), :], at)
        return 0

    def act_tables():
        @pl.when(zz == 0)
        def _():
            kbuf[:, kv_rows(0), :] = jnp.zeros((kvh, tok, HD), kbuf.dtype)
            vbuf[:, kv_rows(0), :] = jnp.zeros((kvh, tok, HD), vbuf.dtype)

        @pl.when(r == 0)
        def _():
            kbuf[:, kv_rows(1), :] = jnp.zeros((kvh, tok, HD), kbuf.dtype)
            vbuf[:, kv_rows(1), :] = jnp.zeros((kvh, tok, HD), vbuf.dtype)

        for c in loc_p:
            c.wait()
        lax.fori_loop(0, 3 * tok // 128, table, 0)

    def prep(i, m_acc):
        cols = pl.ds(pl.multiple_of(i * 384, 128), 384)
        e = ein_ref[:, cols]
        ein_cat[:, cols] = split_cat(e * gain_ref[cols][None, :])
        e = split_cat(e)
        m_hi, m_lo = hi_lo(jnp.broadcast_to(mean_ref[cols][None, :], (16, 384)))
        m_acc = m_acc + dot_nt(m_hi, e) + dot_nt(m_lo, e)
        eout_cat[:, cols] = split_cat(eout_ref[:, cols])
        return m_acc

    def act_prep():
        loc_q.wait()
        lax.fori_loop(0, tok // 128, rot_q, 0)
        for c in loc_k + loc_v:
            c.wait()
        lax.fori_loop(0, tok // 128, rot_own, 0)
        m_acc = lax.fori_loop(0, half // 384, prep, jnp.zeros((16, HD), jnp.float32))
        leave(eout_cat, eout_out)
        st_send[tok:tok + 8, :] = (m_acc + pltpu.roll(m_acc, HD // 2, 1))[0:8]
        code_acc[...] = jnp.zeros_like(code_acc)
        sq_acc[...] = jnp.zeros_like(sq_acc)

    def act_rotk(h):
        wait_kv(r > 0, h, 1)

        def body(i, _):
            at = pl.multiple_of(i * 128, 128)
            krot[h, pl.ds(at, 128), :] = turned(kbuf[h, pl.ds(at, 128), :], at)
            return 0

        lax.fori_loop(0, 2 * tok // 128, body, 0)

    nt = WINDOW // QB + 1
    ri = lax.broadcasted_iota(jnp.int32, (QB, QB), 0)
    ci = lax.broadcasted_iota(jnp.int32, (QB, QB), 1)
    pen = [jnp.where(zz > 0, 0.0, BIG), jnp.where(r > 0, 0.0, BIG), jnp.float32(0.0)]

    def act_G(kv):
        def piece(j, _):
            head, i = (heads // kvh) * kv + j // per, j % per
            rows = pl.ds(pl.multiple_of(i * QB, QB), QB)
            qt = qbuf[rows, pl.ds(pl.multiple_of(head * HD, HD), HD)]
            key_rows = pl.ds(pl.multiple_of(i * QB, QB), nt * QB)
            s = dot_nt(qt, krot[kv, key_rows, :]) * query_scale
            tiles, bias, m = [], [], None
            for t in range(nt):
                st = s[:, t * QB:(t + 1) * QB]
                if t == 0:
                    st = jnp.where(ci > ri, st, -BIG)
                if t == nt - 1:
                    st = jnp.where(ci <= ri, st, -BIG)
                blk = (i + t) // per
                b = jnp.where(blk == 0, pen[0], jnp.where(blk == 1, pen[1], pen[2]))
                mt = jnp.max(st, axis=1, keepdims=True) - b
                m = mt if m is None else jnp.maximum(m, mt)
                tiles.append(st)
                bias.append(b)
            es, tot = [], None
            for st, b in zip(tiles, bias):
                e = jnp.exp(st - (m + b))
                es.append(e)
                se = jnp.sum(e, axis=1, keepdims=True)
                tot = se if tot is None else tot + se
            inv = 1.0 / tot
            p = jnp.concatenate([(e * inv).astype(jnp.bfloat16) for e in es], axis=1)
            o = jnp.dot(p, vbuf[kv, key_rows, :], preferred_element_type=jnp.float32)
            att[rows, pl.ds(pl.multiple_of(f * acols + head * HD, HD), HD)] = o.astype(jnp.bfloat16)
            return 0

        lax.fori_loop(0, (heads // kvh) * per, piece, 0)

    group = heads // kvh * HD
    mine, other = pl.ds(0, tok), pl.ds(tok, tok)

    def att_cols(c, p):
        return pl.ds(pl.multiple_of(c * acols + p * group, 128), group)

    def act_att(p):
        cols = att_cols(f, p)
        send(None, xnb, lambda: (att.at[mine, cols], att.at[other, cols], ar_sem.at[0, p]))
        send(None, part, lambda: (att.at[mine, cols], att.at[mine, cols], ar_sem.at[1, p]))

    def act_attfwd(p):
        cols = att_cols(f, p)
        arrived(att.at[other, cols], ar_sem.at[0, p])
        send(None, part, lambda: (att.at[other, cols], att.at[other, cols], ar_sem.at[2, p]))

    lane = lax.broadcasted_iota(jnp.int32, (tok, HD), 1)
    gained = [False, False]
    mark, drained = [0], [0]

    def hid_cols(k, c):
        return pl.ds(pl.multiple_of(c * pair_w + off[k], 128) if pair[k] else 2 * pair_w + off[k], width[k])

    def stats(k, c):
        cols, w = hid_cols(k, c), width[k]

        def body(i, _):
            rows = pl.ds(pl.multiple_of(i * QB, QB), QB)
            h = hid[rows, cols]
            code_acc[rows, :] += dot_nt(h, ein_cat[:, cols])
            h = h.astype(jnp.float32)
            sq = sq_acc[rows, :]
            for t in range(w // HD):
                ht = h[:, t * HD:(t + 1) * HD]
                sq = sq + ht * ht
            sq_acc[rows, :] = sq
            return 0

        leave(hid.at[:, cols], hid_out.at[:, cols])
        lax.fori_loop(0, per, body, 0)

    def act_mm(k):
        mark[0] = len(pending)
        if not gained[0]:
            gained[0] = True
            for p in range(kvh):
                arrived(att.at[mine, att_cols(1 - f, p)], ar_sem.at[1, p])
        if pair[k] and not gained[1]:
            gained[1] = True
            for p in range(kvh):
                arrived(att.at[other, att_cols(1 - f, p)], ar_sem.at[2, p])
        if both[k]:
            for dz in range(1 - nz, nz):
                for u, skip in ((r + 2 * dz, dz == 0), (2 * (zz + dz) + 1 - yy, False)):
                    if not skip:
                        when(inside(dz), lambda: arrived(wb[k].at[1 - g, u], xr_sem.at[k, u]))
        else:
            for dz in range(1 - nz, nz):
                if dz != 0:
                    act_cross(k, dz)
        wk = wb[k].reshape(2 * acols, width[k])

        def product(at):
            return jnp.dot(att[pl.ds(pl.multiple_of(at, QB), QB), :], wk[...], preferred_element_type=jnp.float32)

        if not pair[k]:
            def body(i, _):
                at = pl.multiple_of(i * QB, QB)
                hid[pl.ds(at, QB), hid_cols(k, g)] = product(at).astype(jnp.bfloat16)
                return 0

            lax.fori_loop(0, per, body, 0)
            stats(k, g)
        else:
            cols = slice(off[k], off[k] + width[k])

            def body(i, _):
                n = jnp.where(i < per, i, i - per)
                at = pl.multiple_of(n * QB, QB)
                d = product(jnp.where(i < per, tok, 0) + at).astype(jnp.bfloat16)

                @pl.when(i < per)
                def _():
                    hsend[pl.ds(at, QB), cols] = d

                def ends(j):
                    rows = pl.ds(j * QB, QB)
                    return hsend.at[rows, cols], hid.at[rows, hid_cols(k, g)], hr_sem.at[k, j]

                for j in range(per):
                    send(i == j, xnb, ends, j)
                    pending[-1] = (None, pending[-1][1])

                @pl.when(i >= per)
                def _():
                    hid[pl.ds(at, QB), hid_cols(k, g)] = d
                return 0

            lax.fori_loop(0, 2 * per, body, 0)
            stats(k, g)

    def act_hid(k):
        for j in range(per):
            arrived(hid.at[pl.ds(j * QB, QB), hid_cols(k, 1 - g)], hr_sem.at[k, j])
        stats(k, 1 - g)

    def drain(end):
        for cond, make in pending[drained[0]:end]:
            when(cond, lambda make=make: make().wait_send())
        drained[0] = end

    def act_drain():
        drain(mark[0])

    acts = {"drain": act_drain, "own": act_own, "line": act_line, "cross": act_cross, "kvup": act_kvup, "kvy": act_kvy,
            "kvrelay": act_kvrelay, "tables": act_tables, "prep": act_prep, "rotk": act_rotk, "G": act_G,
            "att": act_att, "attfwd": act_attfwd, "mm": act_mm, "hid": act_hid}
    for name, *rest in ORDER if nz == 4 else plain_order(kinds, nz, kvh):
        acts[name](*rest)

    code = code_acc[...]
    code = code + pltpu.roll(code, HD // 2, 1)
    sq = jnp.sum(sq_acc[...], axis=1, keepdims=True)
    st_send[0:tok, :] = jnp.where(lane < HD // 2, code, sq)
    swap = pltpu.make_async_remote_copy(src_ref=st_send, dst_ref=st_recv, send_sem=st_sem.at[0], recv_sem=st_sem.at[1],
                                        device_id=part, device_id_type=MESH)
    swap.start()
    drain(len(pending))
    swap.wait()
    sums = st_send[0:tok, :] + st_recv[0:tok, :]
    turned_sums = pltpu.roll(sums, HD // 2, 1)
    code = jnp.where(lane < HD // 2, sums, turned_sums)
    total = jnp.where(lane < HD // 2, turned_sums, sums)
    inv_rms = lax.rsqrt(total * (1.0 / d_full) + norm_eps)
    mean_sum = st_send[tok:tok + 1, :] + st_recv[tok:tok + 1, :]
    c_hi, c_lo = hi_lo(inv_rms * code - mean_sum)
    c_ref[:, 0:HD] = c_hi
    c_ref[:, HD:2 * HD] = c_lo
    scale_ref[...] = inv_rms
    for c in left:
        c.wait()


def finish(c_hbm, scale_hbm, gain_hbm, hid_hbm, eout_hbm, out_hbm, c_ref, scale_ref, gain_ref, hid, eout, out, in_sem,
           out_sem):
    n = hid.shape[1] // TN

    def cols(i):
        return pl.ds(i * TN, TN)

    def come(i):
        return (pltpu.make_async_copy(eout_hbm.at[:, cols(i)], eout.at[:, cols(i)], in_sem.at[i]),
                pltpu.make_async_copy(hid_hbm.at[:, cols(i)], hid.at[:, cols(i)], in_sem.at[n + i]))

    def go(i):
        return pltpu.make_async_copy(out.at[:, cols(i)], out_hbm.at[:, cols(i)], out_sem.at[i])

    first = [pltpu.make_async_copy(src, dst, in_sem.at[2 * n + j]) for j, (src, dst) in enumerate(
        ((c_hbm, c_ref), (scale_hbm, scale_ref), (gain_hbm, gain_ref)))]
    for c in first:
        c.start()
    for i in range(n):
        for c in come(i):
            c.start()
    for c in first:
        c.wait()

    def body(i):
        for c in come(i):
            c.wait()
        e = eout[:, cols(i)]
        back = jnp.dot(c_ref[...], jnp.concatenate([e, e], axis=0), preferred_element_type=jnp.float32)
        h = hid[:, cols(i)].astype(jnp.float32) * jnp.concatenate([scale_ref[...]] * (TN // HD), axis=1)
        out[:, cols(i)] = (h * gain_ref[cols(i)][None, :] - back).astype(jnp.bfloat16)
        go(i).start()

    for i in range(n):
        body(i)
    for i in range(n):
        go(i).wait()


def solution(mesh):
    n_row = mesh.shape["row"]

    def on_device(queries, keys, values, out_proj, post_gain, mean_vec, erase_in, erase_out):
        tok = queries.shape[0]
        rows, d_full = out_proj.shape
        half = post_gain.shape[0]
        half_dim = HD // 2
        kvh = keys.shape[1] // HD
        inverse = np.exp(-(2.0 * np.arange(half_dim, dtype=np.float32) / HD) * np.log(np.float32(rope_base)))
        inverse = np.concatenate([inverse, inverse]).astype(np.float32)[None, :]
        any_spec = pl.BlockSpec(memory_space=pltpu.HBM)
        vm = pl.BlockSpec(memory_space=pltpu.VMEM)
        kinds, width, off, pair_w, rest_w, via_z = plan(n_row)
        n_chunk = len(kinds)
        hops = n_row // 2 - 1
        n_ss = sum(6 + 4 * hops + (b == "both") * (4 * hops + 1) + tok // QB for b in kinds) + 9 * kvh
        bf, f32 = jnp.bfloat16, jnp.float32
        dma = pltpu.SemaphoreType.DMA
        hidden, writing, code, scale = pl.pallas_call(
            functools.partial(kernel, n_row, d_full, n_ss),
            out_shape=[jax.ShapeDtypeStruct((tok, half), bf), jax.ShapeDtypeStruct((HD, half), bf),
                       jax.ShapeDtypeStruct((tok, 2 * HD), bf), jax.ShapeDtypeStruct((tok, HD), f32)],
            in_specs=[any_spec] * 9,
            out_specs=[pl.BlockSpec(memory_space=pl.ANY)] * 2 + [vm, vm],
            scratch_shapes=[pltpu.VMEM((2, n_row, rows, w), bf) for w in width] + [
                pltpu.VMEM(queries.shape, bf),
                pltpu.VMEM((kvh, 3 * tok, HD), bf),
                pltpu.VMEM((kvh, 3 * tok, HD), bf),
                pltpu.VMEM((kvh, 3 * tok, HD), bf),
                pltpu.VMEM((2 * tok, 2 * queries.shape[1]), bf),
                pltpu.VMEM((tok, half), bf),
                pltpu.VMEM((tok, pair_w), bf),
                pltpu.VMEM((3 * tok, HD), f32),
                pltpu.VMEM((3 * tok, HD), f32),
                pltpu.VMEM((HD, half), bf),
                pltpu.VMEM((HD, half), bf),
                pltpu.VMEM((tok, HD), f32),
                pltpu.VMEM((tok, HD), f32),
                pltpu.VMEM((tok + 8, HD), f32),
                pltpu.VMEM((tok + 8, HD), f32),
                pltpu.VMEM((half,), f32),
                pltpu.VMEM((half,), f32),
                pltpu.VMEM((erase_in.shape[1], half), f32),
                pltpu.VMEM((erase_in.shape[1], half), f32),
                pltpu.VMEM((1, HD), f32),
                dma((n_chunk + 2 * kvh + 6,)), dma((n_ss,)), dma((n_chunk, n_row)), dma((n_chunk, n_row)),
                dma((n_chunk,)), dma((2, kvh, 2)), dma((3, kvh)), dma((n_chunk, tok // QB)), dma((2,)),
                dma((1 + sum(2 if b == "pair" else 1 for b in kinds),)),
            ],
            compiler_params=pltpu.CompilerParams(
                collective_id=0, has_side_effects=True, vmem_limit_bytes=60 * 1024 * 1024),
        )(queries, keys, values, out_proj, post_gain, mean_vec,
          erase_in.T, erase_out.T, jnp.asarray(inverse))
        return pl.pallas_call(
            finish,
            out_shape=jax.ShapeDtypeStruct((tok, half), bf),
            in_specs=[any_spec] * 5,
            out_specs=any_spec,
            scratch_shapes=[
                pltpu.VMEM((tok, 2 * HD), bf), pltpu.VMEM((tok, HD), f32), pltpu.VMEM((half,), f32),
                pltpu.VMEM((tok, half), bf), pltpu.VMEM((HD, half), bf), pltpu.VMEM((tok, half), bf),
                dma((2 * half // TN + 3,)), dma((half // TN,)),
            ],
            compiler_params=pltpu.CompilerParams(vmem_limit_bytes=60 * 1024 * 1024),
        )(code, scale, post_gain, hidden, writing)

    placed = (
        P(("grp", "row"), "col"),
        P(("grp", "row"), "col"),
        P(("grp", "row"), "col"),
        P(("col", "row"), None),
        P("col"),
        P("col"),
        P("col", None),
        P("col", None),
    )
    return jax.shard_map(
        on_device, mesh=mesh, in_specs=placed, out_specs=P(("grp", "row"), "col"), check_vma=False
    )
```

```python
import functools

import jax
import jax.numpy as jnp
import numpy as np
from jax import lax
from jax.experimental import pallas as pl
from jax.experimental.pallas import tpu as pltpu
from jax.sharding import PartitionSpec as P

HD = 128
WINDOW = 1024
MESH = pl.DeviceIdType.MESH
query_scale = 168.0 ** (-0.5)
norm_eps = 1e-06
rope_base = 10000.0
QB = 256
BLOCKS = (384, 768, 1024, 512)
BIG = 1e30

CHUNKS = (("own", 128), ("pair", 512), ("pair", 256), ("pair", 256), ("pair", 256))
VIA_Z = (0, 3, 4)
ORDER = (
    ("kvup", 2), ("kvup", 3), ("kvup", 1), ("kvy", 2), ("kvup", 0), ("kvy", 3), ("own", 1), ("own", 2), ("tables",),
    ("line", 1, 1), ("kvrelay", 2), ("prep",), ("kvy", 1), ("line", 2, 1), ("rotk", 2), ("kvrelay", 3), ("G", 2),
    ("rotk", 3), ("att", 2), ("kvy", 0), ("cross", 1, 0), ("kvrelay", 1), ("G", 3), ("kvrelay", 0), ("att", 3),
    ("rotk", 1), ("line", 1, -1), ("line", 1, 2), ("own", 3), ("cross", 2, 0), ("G", 1), ("att", 1), ("rotk", 0),
    ("G", 0), ("line", 1, -2), ("own", 0), ("att", 0), ("line", 3, 1), ("attfwd", 1), ("line", 1, -3),
    ("line", 3, -1), ("line", 1, 3), ("line", 2, -1), ("line", 0, 1), ("own", 4), ("attfwd", 2), ("line", 2, 2),
    ("attfwd", 3), ("attfwd", 0), ("line", 3, 2), ("line", 2, -2), ("mm", 1), ("line", 2, -3), ("line", 3, -2),
    ("line", 4, 1), ("line", 4, -1), ("cross", 3, 0), ("line", 3, -3), ("line", 2, 3), ("line", 3, 3), ("line", 4, 2),
    ("line", 4, -2), ("line", 0, 2), ("line", 0, -1), ("cross", 4, 0), ("cross", 0, 0), ("mm", 2), ("hid", 1),
    ("line", 4, -3), ("line", 4, 3), ("mm", 3), ("line", 0, 3), ("line", 0, -2), ("mm", 4), ("hid", 3),
    ("line", 0, -3), ("hid", 2), ("mm", 0), ("drain",), ("hid", 4),
)


def plain_order(kinds, nz, kvh):
    n_chunk = len(kinds)
    out = [("own", k) for k in range(n_chunk)]
    out += [(a, h) for h in range(kvh) for a in ("kvup", "kvy")]
    out += [("tables",), ("prep",)]
    out += [("kvrelay", h) for h in range(kvh)]
    for k in range(n_chunk):
        for d in range(1, nz):
            out += [("line", k, -d), ("line", k, d)]
        out += [("cross", k, 0)]
        if kinds[k] == "both":
            out += [("cross", k, d) for e in range(1, nz) for d in (-e, e)]
    for p in range(kvh):
        out += [("rotk", p), ("G", p), ("att", p)]
    out += [("attfwd", p) for p in range(kvh)]
    out += [("mm", k) for k in range(n_chunk)]
    out += [("hid", k) for k in range(n_chunk) if kinds[k] == "pair"]
    return out


def split_cat(x):
    hi = x.astype(jnp.bfloat16).astype(jnp.float32)
    return jnp.concatenate([hi, x - hi], axis=0).astype(jnp.bfloat16)


def hi_lo(x):
    hi = x.astype(jnp.bfloat16)
    return hi, (x - hi.astype(jnp.float32)).astype(jnp.bfloat16)


def dot_nt(x, y):
    return lax.dot_general(x, y, (((1,), (1,)), ((), ())), preferred_element_type=jnp.float32)


def plan(n_row):
    nz = n_row // 2
    chunks = CHUNKS if nz == 4 else (("both", 384), ("pair", 1152))
    via_z = VIA_Z if nz == 4 else (0,)
    kinds = [c[0] for c in chunks]
    width = [c[1] for c in chunks]
    off, pair_w, rest_w = [], 0, 0
    for kind, w in chunks:
        off.append(pair_w if kind == "pair" else rest_w)
        pair_w, rest_w = (pair_w + w, rest_w) if kind == "pair" else (pair_w, rest_w + w)
    return kinds, width, off, pair_w, rest_w, via_z


def kernel(n_row, d_full, n_ss, q_hbm, k_hbm, v_hbm, w_hbm, *rest):
    params_hbm, rest = rest[:5], rest[5:]
    hid_out, eout_out, c_ref, scale_ref, *scratch = rest
    kinds, width, off, pair_w, rest_w, via_z = plan(n_row)
    n_chunk = len(kinds)
    pair, both = [c == "pair" for c in kinds], [c == "both" for c in kinds]
    wb = scratch[:n_chunk]
    (qbuf, kbuf, vbuf, krot, att, hid, hsend, cosb, sinb, ein_cat, eout_cat, code_acc, sq_acc, st_send, st_recv,
     gain_ref, mean_ref, ein_ref, eout_ref, inv_ref, loc_sem, ss_sem, wr_sem, xr_sem, cr_sem, kr_sem, ar_sem, hr_sem, st_sem, out_sem) = scratch[n_chunk:]
    nz = n_row // 2
    g, r, f = lax.axis_index("grp"), lax.axis_index("row"), lax.axis_index("col")
    zz, yy = r // 2, r % 2
    has_up, has_dn = zz < nz - 1, zz > 0
    tok = qbuf.shape[0]
    half = pair_w * 2 + rest_w
    kvh = kbuf.shape[0]
    heads = qbuf.shape[1] // HD
    acols = heads * HD
    per = tok // QB

    part = {"grp": g, "row": r, "col": 1 - f}
    xnb = {"grp": 1 - g, "row": r, "col": f}
    ynb = {"grp": g, "row": 2 * zz + 1 - yy, "col": f}
    up = {"grp": g, "row": r + 2, "col": f}
    dn = {"grp": g, "row": r - 2, "col": f}

    barrier = pltpu.get_barrier_semaphore()
    for nb in (part, xnb, ynb):
        pl.semaphore_signal(barrier, inc=1, device_id=nb, device_id_type=MESH)

    @pl.when(has_up)
    def _():
        pl.semaphore_signal(barrier, inc=1, device_id=up, device_id_type=MESH)

    @pl.when(has_dn)
    def _():
        pl.semaphore_signal(barrier, inc=1, device_id=dn, device_id_type=MESH)

    def own_w(k, c):
        at = c * half + (g * pair_w + off[k] if pair[k] else 2 * pair_w + off[k])
        return w_hbm.at[:, pl.ds(pl.multiple_of(at, 128), width[k])]

    def head_cols(h):
        return pl.ds(h * HD, HD)

    own_rows = pl.ds(2 * tok, tok)
    loc_w = [pltpu.make_async_copy(own_w(k, f), wb[k].at[f, r], loc_sem.at[k]) for k in range(n_chunk)]
    loc_k = [pltpu.make_async_copy(k_hbm.at[:, head_cols(h)], kbuf.at[h, own_rows, :], loc_sem.at[n_chunk + h])
             for h in range(kvh)]
    loc_v = [pltpu.make_async_copy(v_hbm.at[:, head_cols(h)], vbuf.at[h, own_rows, :], loc_sem.at[n_chunk + kvh + h])
             for h in range(kvh)]
    loc_q = pltpu.make_async_copy(q_hbm, qbuf, loc_sem.at[n_chunk + 2 * kvh])
    loc_p = [pltpu.make_async_copy(src, dst, loc_sem.at[n_chunk + 2 * kvh + 1 + i]) for i, (src, dst) in enumerate(
        zip(params_hbm, (gain_ref, mean_ref, ein_ref, eout_ref, inv_ref)))]
    for c in loc_w + loc_k + loc_v + [loc_q] + loc_p:
        c.start()

    pl.semaphore_wait(barrier, 3 + has_up.astype(jnp.int32) + has_dn.astype(jnp.int32))

    pending = []
    left = []

    def leave(src, dst):
        c = pltpu.make_async_copy(src, dst, out_sem.at[len(left)])
        left.append(c)
        c.start()

    def send(cond, dev, ends, *args):
        i = len(pending)
        assert i < n_ss, i

        def make():
            src, dst, recv = ends(*args)
            return pltpu.make_async_remote_copy(
                src_ref=src, dst_ref=dst, send_sem=ss_sem.at[i], recv_sem=recv, device_id=dev, device_id_type=MESH)

        pending.append((cond, make))
        if cond is None:
            make().start()
        else:
            @pl.when(cond)
            def _():
                make().start()

    def when(cond, fn):
        if cond is None:
            fn()
        else:
            pl.when(cond)(fn)

    def arrived(ref, sem):
        pltpu.make_async_copy(ref, ref, sem).wait()

    for k in range(n_chunk):
        send(None, part, lambda k: (own_w(k, 1 - f), wb[k].at[f, r], cr_sem.at[k]), k)

    def block(k, u):
        return wb[k].at[g, u] if both[k] else wb[k].at[:, u]

    def send_w(cond, k, u, dev):
        send(cond, dev, lambda: (block(k, u), block(k, u), wr_sem.at[k, u]))

    def send_x(cond, k, u):
        send(cond, xnb, lambda: (wb[k].at[g, u], wb[k].at[g, u], xr_sem.at[k, u]))

    def act_own(k):
        loc_w[k].wait()
        arrived(wb[k].at[1 - f, r], cr_sem.at[k])
        send_w(has_up, k, r, up)
        send_w(has_dn, k, r, dn)
        send_w(None, k, r, ynb)

    def inside(dz):
        return None if dz == 0 else (zz + dz >= 0 if dz < 0 else zz + dz < nz)

    def act_line(k, dz):
        cond, u = inside(dz), r + 2 * dz
        when(cond, lambda: arrived(block(k, u), wr_sem.at[k, u]))
        if dz < 0:
            send_w(cond & has_up, k, u, up)
        else:
            send_w(cond & has_dn, k, u, dn)
        if dz != 1:
            send_w(cond & has_up if dz == -1 and k in via_z else cond, k, u, ynb)
        if both[k]:
            send_x(cond, k, u)

    def act_cross(k, dz):
        cond, u = inside(dz), 2 * (zz + dz) + 1 - yy
        when(cond, lambda: arrived(block(k, u), wr_sem.at[k, u]))
        if dz == 0:
            send_w(has_dn, k, u, dn)
            if k in via_z:
                send_w(zz == nz - 2, k, u, up)
        if both[k]:
            send_x(cond, k, u)

    def kv_rows(slot):
        return pl.ds(slot * tok, tok)

    def send_kv(cond, h, src_slot, slot, dev):
        def ends(n):
            hbm, buf = ((k_hbm, kbuf), (v_hbm, vbuf))[n]
            src = hbm.at[:, head_cols(h)] if src_slot == 2 else buf.at[h, kv_rows(src_slot), :]
            return src, buf.at[h, kv_rows(slot), :], kr_sem.at[slot, h, n]

        for n in range(2):
            send(cond, dev, ends, n)

    def wait_kv(cond, h, slot):
        @pl.when(cond)
        def _():
            for n, buf in enumerate((kbuf, vbuf)):
                arrived(buf.at[h, kv_rows(slot), :], kr_sem.at[slot, h, n])

    def act_kvup(h):
        send_kv(has_up, h, 2, 0, up)

    def act_kvy(h):
        send_kv(yy == 0, h, 2, 1, ynb)

    def act_kvrelay(h):
        wait_kv(has_dn, h, 0)
        send_kv(has_dn & (yy == 1), h, 0, 1, ynb)

    sign = jnp.where(lax.broadcasted_iota(jnp.int32, (1, HD), 1) < HD // 2, -1.0, 1.0)
    key_base = r * tok - 2 * tok

    def table(i, _):
        at = pl.multiple_of(i * 128, 128)
        pos = (key_base + at + lax.broadcasted_iota(jnp.int32, (128, HD), 0)).astype(jnp.float32)
        ang = pos * inv_ref[...]
        cosb[pl.ds(at, 128), :] = jnp.cos(ang)
        sinb[pl.ds(at, 128), :] = jnp.sin(ang) * sign
        return 0

    def turned(x, at):
        x = x.astype(jnp.float32)
        cs, sn = cosb[pl.ds(at, 128), :], sinb[pl.ds(at, 128), :]
        return (x * cs + pltpu.roll(x, HD // 2, 1) * sn).astype(jnp.bfloat16)

    def rot_q(i, _):
        at = pl.multiple_of(i * 128, 128)
        for h in range(heads):
            cols = slice(h * HD, (h + 1) * HD)
            qbuf[pl.ds(at, 128), cols] = turned(qbuf[pl.ds(at, 128), cols], 2 * tok + at)
        return 0

    def rot_own(i, _):
        at = pl.multiple_of(2 * tok + i * 128, 128)
        for h in range(kvh):
            krot[h, pl.ds(at, 128), :] = turned(kbuf[h, pl.ds(at, 128), :], at)
        return 0

    def act_tables():
        @pl.when(zz == 0)
        def _():
            kbuf[:, kv_rows(0), :] = jnp.zeros((kvh, tok, HD), kbuf.dtype)
            vbuf[:, kv_rows(0), :] = jnp.zeros((kvh, tok, HD), vbuf.dtype)

        @pl.when(r == 0)
        def _():
            kbuf[:, kv_rows(1), :] = jnp.zeros((kvh, tok, HD), kbuf.dtype)
            vbuf[:, kv_rows(1), :] = jnp.zeros((kvh, tok, HD), vbuf.dtype)

        for c in loc_p:
            c.wait()
        lax.fori_loop(0, 3 * tok // 128, table, 0)

    def prep(i, m_acc):
        cols = pl.ds(pl.multiple_of(i * 384, 128), 384)
        e = ein_ref[:, cols]
        ein_cat[:, cols] = split_cat(e * gain_ref[cols][None, :])
        e = split_cat(e)
        m_hi, m_lo = hi_lo(jnp.broadcast_to(mean_ref[cols][None, :], (16, 384)))
        m_acc = m_acc + dot_nt(m_hi, e) + dot_nt(m_lo, e)
        eout_cat[:, cols] = split_cat(eout_ref[:, cols])
        return m_acc

    def act_prep():
        loc_q.wait()
        lax.fori_loop(0, tok // 128, rot_q, 0)
        for c in loc_k + loc_v:
            c.wait()
        lax.fori_loop(0, tok // 128, rot_own, 0)
        m_acc = lax.fori_loop(0, half // 384, prep, jnp.zeros((16, HD), jnp.float32))
        leave(eout_cat, eout_out)
        st_send[tok:tok + 8, :] = (m_acc + pltpu.roll(m_acc, HD // 2, 1))[0:8]
        code_acc[...] = jnp.zeros_like(code_acc)
        sq_acc[...] = jnp.zeros_like(sq_acc)

    def act_rotk(h):
        wait_kv(r > 0, h, 1)

        def body(i, _):
            at = pl.multiple_of(i * 128, 128)
            krot[h, pl.ds(at, 128), :] = turned(kbuf[h, pl.ds(at, 128), :], at)
            return 0

        lax.fori_loop(0, 2 * tok // 128, body, 0)

    nt = WINDOW // QB + 1
    ri = lax.broadcasted_iota(jnp.int32, (QB, QB), 0)
    ci = lax.broadcasted_iota(jnp.int32, (QB, QB), 1)
    pen = [jnp.where(zz > 0, 0.0, BIG), jnp.where(r > 0, 0.0, BIG), jnp.float32(0.0)]

    def act_G(kv):
        def piece(j, _):
            head, i = (heads // kvh) * kv + j // per, j % per
            rows = pl.ds(pl.multiple_of(i * QB, QB), QB)
            qt = qbuf[rows, pl.ds(pl.multiple_of(head * HD, HD), HD)]
            key_rows = pl.ds(pl.multiple_of(i * QB, QB), nt * QB)
            s = dot_nt(qt, krot[kv, key_rows, :]) * query_scale
            tiles, bias, m = [], [], None
            for t in range(nt):
                st = s[:, t * QB:(t + 1) * QB]
                if t == 0:
                    st = jnp.where(ci > ri, st, -BIG)
                if t == nt - 1:
                    st = jnp.where(ci <= ri, st, -BIG)
                blk = (i + t) // per
                b = jnp.where(blk == 0, pen[0], jnp.where(blk == 1, pen[1], pen[2]))
                mt = jnp.max(st, axis=1, keepdims=True) - b
                m = mt if m is None else jnp.maximum(m, mt)
                tiles.append(st)
                bias.append(b)
            es, tot = [], None
            for st, b in zip(tiles, bias):
                e = jnp.exp(st - (m + b))
                es.append(e)
                se = jnp.sum(e, axis=1, keepdims=True)
                tot = se if tot is None else tot + se
            inv = 1.0 / tot
            p = jnp.concatenate([(e * inv).astype(jnp.bfloat16) for e in es], axis=1)
            o = jnp.dot(p, vbuf[kv, key_rows, :], preferred_element_type=jnp.float32)
            att[rows, pl.ds(pl.multiple_of(f * acols + head * HD, HD), HD)] = o.astype(jnp.bfloat16)
            return 0

        lax.fori_loop(0, (heads // kvh) * per, piece, 0)

    group = heads // kvh * HD
    mine, other = pl.ds(0, tok), pl.ds(tok, tok)

    def att_cols(c, p):
        return pl.ds(pl.multiple_of(c * acols + p * group, 128), group)

    def act_att(p):
        cols = att_cols(f, p)
        send(None, xnb, lambda: (att.at[mine, cols], att.at[other, cols], ar_sem.at[0, p]))
        send(None, part, lambda: (att.at[mine, cols], att.at[mine, cols], ar_sem.at[1, p]))

    def act_attfwd(p):
        cols = att_cols(f, p)
        arrived(att.at[other, cols], ar_sem.at[0, p])
        send(None, part, lambda: (att.at[other, cols], att.at[other, cols], ar_sem.at[2, p]))

    lane = lax.broadcasted_iota(jnp.int32, (tok, HD), 1)
    gained = [False, False]
    mark, drained = [0], [0]

    def hid_cols(k, c):
        return pl.ds(pl.multiple_of(c * pair_w + off[k], 128) if pair[k] else 2 * pair_w + off[k], width[k])

    def stats(k, c):
        cols, w = hid_cols(k, c), width[k]

        def body(i, _):
            rows = pl.ds(pl.multiple_of(i * QB, QB), QB)
            h = hid[rows, cols]
            code_acc[rows, :] += dot_nt(h, ein_cat[:, cols])
            h = h.astype(jnp.float32)
            sq = sq_acc[rows, :]
            for t in range(w // HD):
                ht = h[:, t * HD:(t + 1) * HD]
                sq = sq + ht * ht
            sq_acc[rows, :] = sq
            return 0

        leave(hid.at[:, cols], hid_out.at[:, cols])
        lax.fori_loop(0, per, body, 0)

    def act_mm(k):
        mark[0] = len(pending)
        if not gained[0]:
            gained[0] = True
            for p in range(kvh):
                arrived(att.at[mine, att_cols(1 - f, p)], ar_sem.at[1, p])
        if pair[k] and not gained[1]:
            gained[1] = True
            for p in range(kvh):
                arrived(att.at[other, att_cols(1 - f, p)], ar_sem.at[2, p])
        if both[k]:
            for dz in range(1 - nz, nz):
                for u, skip in ((r + 2 * dz, dz == 0), (2 * (zz + dz) + 1 - yy, False)):
                    if not skip:
                        when(inside(dz), lambda: arrived(wb[k].at[1 - g, u], xr_sem.at[k, u]))
        else:
            for dz in range(1 - nz, nz):
                if dz != 0:
                    act_cross(k, dz)
        wk = wb[k].reshape(2 * acols, width[k])

        def product(at):
            return jnp.dot(att[pl.ds(pl.multiple_of(at, QB), QB), :], wk[...], preferred_element_type=jnp.float32)

        if not pair[k]:
            def body(i, _):
                at = pl.multiple_of(i * QB, QB)
                hid[pl.ds(at, QB), hid_cols(k, g)] = product(at).astype(jnp.bfloat16)
                return 0

            lax.fori_loop(0, per, body, 0)
            stats(k, g)
        else:
            cols = slice(off[k], off[k] + width[k])

            def body(i, _):
                n = jnp.where(i < per, i, i - per)
                at = pl.multiple_of(n * QB, QB)
                d = product(jnp.where(i < per, tok, 0) + at).astype(jnp.bfloat16)

                @pl.when(i < per)
                def _():
                    hsend[pl.ds(at, QB), cols] = d

                def ends(j):
                    rows = pl.ds(j * QB, QB)
                    return hsend.at[rows, cols], hid.at[rows, hid_cols(k, g)], hr_sem.at[k, j]

                for j in range(per):
                    send(i == j, xnb, ends, j)
                    pending[-1] = (None, pending[-1][1])

                @pl.when(i >= per)
                def _():
                    hid[pl.ds(at, QB), hid_cols(k, g)] = d
                return 0

            lax.fori_loop(0, 2 * per, body, 0)
            stats(k, g)

    def act_hid(k):
        for j in range(per):
            arrived(hid.at[pl.ds(j * QB, QB), hid_cols(k, 1 - g)], hr_sem.at[k, j])
        stats(k, 1 - g)

    def drain(end):
        for cond, make in pending[drained[0]:end]:
            when(cond, lambda make=make: make().wait_send())
        drained[0] = end

    def act_drain():
        drain(mark[0])

    acts = {"drain": act_drain, "own": act_own, "line": act_line, "cross": act_cross, "kvup": act_kvup, "kvy": act_kvy,
            "kvrelay": act_kvrelay, "tables": act_tables, "prep": act_prep, "rotk": act_rotk, "G": act_G,
            "att": act_att, "attfwd": act_attfwd, "mm": act_mm, "hid": act_hid}
    for name, *rest in ORDER if nz == 4 else plain_order(kinds, nz, kvh):
        acts[name](*rest)

    code = code_acc[...]
    code = code + pltpu.roll(code, HD // 2, 1)
    sq = jnp.sum(sq_acc[...], axis=1, keepdims=True)
    st_send[0:tok, :] = jnp.where(lane < HD // 2, code, sq)
    swap = pltpu.make_async_remote_copy(src_ref=st_send, dst_ref=st_recv, send_sem=st_sem.at[0], recv_sem=st_sem.at[1],
                                        device_id=part, device_id_type=MESH)
    swap.start()
    drain(len(pending))
    swap.wait()
    sums = st_send[0:tok, :] + st_recv[0:tok, :]
    turned_sums = pltpu.roll(sums, HD // 2, 1)
    code = jnp.where(lane < HD // 2, sums, turned_sums)
    total = jnp.where(lane < HD // 2, turned_sums, sums)
    inv_rms = lax.rsqrt(total * (1.0 / d_full) + norm_eps)
    mean_sum = st_send[tok:tok + 1, :] + st_recv[tok:tok + 1, :]
    c_hi, c_lo = hi_lo(inv_rms * code - mean_sum)
    c_ref[:, 0:HD] = c_hi
    c_ref[:, HD:2 * HD] = c_lo
    scale_ref[...] = inv_rms
    for c in left:
        c.wait()


def finish(c_hbm, scale_hbm, gain_hbm, hid_hbm, eout_hbm, out_hbm, c_ref, scale_ref, gain_ref, hid, eout, out, in_sem,
           out_sem):
    n = len(BLOCKS)

    def cols(i):
        return pl.ds(sum(BLOCKS[:i]), BLOCKS[i])

    def come(i):
        return (pltpu.make_async_copy(eout_hbm.at[:, cols(i)], eout.at[:, cols(i)], in_sem.at[i]),
                pltpu.make_async_copy(hid_hbm.at[:, cols(i)], hid.at[:, cols(i)], in_sem.at[n + i]))

    def go(i):
        return pltpu.make_async_copy(out.at[:, cols(i)], out_hbm.at[:, cols(i)], out_sem.at[i])

    first = [pltpu.make_async_copy(src, dst, in_sem.at[2 * n + j]) for j, (src, dst) in enumerate(
        ((c_hbm, c_ref), (scale_hbm, scale_ref), (gain_hbm, gain_ref)))]
    for c in first:
        c.start()
    for i in range(n):
        for c in come(i):
            c.start()
    for c in first:
        c.wait()

    def body(i):
        for c in come(i):
            c.wait()
        e = eout[:, cols(i)]
        back = jnp.dot(c_ref[...], jnp.concatenate([e, e], axis=0), preferred_element_type=jnp.float32)
        h = hid[:, cols(i)].astype(jnp.float32) * jnp.concatenate([scale_ref[...]] * (BLOCKS[i] // HD), axis=1)
        out[:, cols(i)] = (h * gain_ref[cols(i)][None, :] - back).astype(jnp.bfloat16)
        go(i).start()

    for i in range(n):
        body(i)
    for i in range(n):
        go(i).wait()


def solution(mesh):
    n_row = mesh.shape["row"]

    def on_device(queries, keys, values, out_proj, post_gain, mean_vec, erase_in, erase_out):
        tok = queries.shape[0]
        rows, d_full = out_proj.shape
        half = post_gain.shape[0]
        half_dim = HD // 2
        kvh = keys.shape[1] // HD
        inverse = np.exp(-(2.0 * np.arange(half_dim, dtype=np.float32) / HD) * np.log(np.float32(rope_base)))
        inverse = np.concatenate([inverse, inverse]).astype(np.float32)[None, :]
        any_spec = pl.BlockSpec(memory_space=pltpu.HBM)
        vm = pl.BlockSpec(memory_space=pltpu.VMEM)
        kinds, width, off, pair_w, rest_w, via_z = plan(n_row)
        n_chunk = len(kinds)
        hops = n_row // 2 - 1
        n_ss = sum(6 + 4 * hops + (b == "both") * (4 * hops + 1) + tok // QB for b in kinds) + 9 * kvh
        bf, f32 = jnp.bfloat16, jnp.float32
        dma = pltpu.SemaphoreType.DMA
        hidden, writing, code, scale = pl.pallas_call(
            functools.partial(kernel, n_row, d_full, n_ss),
            out_shape=[jax.ShapeDtypeStruct((tok, half), bf), jax.ShapeDtypeStruct((HD, half), bf),
                       jax.ShapeDtypeStruct((tok, 2 * HD), bf), jax.ShapeDtypeStruct((tok, HD), f32)],
            in_specs=[any_spec] * 9,
            out_specs=[pl.BlockSpec(memory_space=pl.ANY)] * 2 + [vm, vm],
            scratch_shapes=[pltpu.VMEM((2, n_row, rows, w), bf) for w in width] + [
                pltpu.VMEM(queries.shape, bf),
                pltpu.VMEM((kvh, 3 * tok, HD), bf),
                pltpu.VMEM((kvh, 3 * tok, HD), bf),
                pltpu.VMEM((kvh, 3 * tok, HD), bf),
                pltpu.VMEM((2 * tok, 2 * queries.shape[1]), bf),
                pltpu.VMEM((tok, half), bf),
                pltpu.VMEM((tok, pair_w), bf),
                pltpu.VMEM((3 * tok, HD), f32),
                pltpu.VMEM((3 * tok, HD), f32),
                pltpu.VMEM((HD, half), bf),
                pltpu.VMEM((HD, half), bf),
                pltpu.VMEM((tok, HD), f32),
                pltpu.VMEM((tok, HD), f32),
                pltpu.VMEM((tok + 8, HD), f32),
                pltpu.VMEM((tok + 8, HD), f32),
                pltpu.VMEM((half,), f32),
                pltpu.VMEM((half,), f32),
                pltpu.VMEM((erase_in.shape[1], half), f32),
                pltpu.VMEM((erase_in.shape[1], half), f32),
                pltpu.VMEM((1, HD), f32),
                dma((n_chunk + 2 * kvh + 6,)), dma((n_ss,)), dma((n_chunk, n_row)), dma((n_chunk, n_row)),
                dma((n_chunk,)), dma((2, kvh, 2)), dma((3, kvh)), dma((n_chunk, tok // QB)), dma((2,)),
                dma((1 + sum(2 if b == "pair" else 1 for b in kinds),)),
            ],
            compiler_params=pltpu.CompilerParams(
                collective_id=0, has_side_effects=True, vmem_limit_bytes=60 * 1024 * 1024),
        )(queries, keys, values, out_proj, post_gain, mean_vec,
          erase_in.T, erase_out.T, jnp.asarray(inverse))
        return pl.pallas_call(
            finish,
            out_shape=jax.ShapeDtypeStruct((tok, half), bf),
            in_specs=[any_spec] * 5,
            out_specs=any_spec,
            scratch_shapes=[
                pltpu.VMEM((tok, 2 * HD), bf), pltpu.VMEM((tok, HD), f32), pltpu.VMEM((half,), f32),
                pltpu.VMEM((tok, half), bf), pltpu.VMEM((HD, half), bf), pltpu.VMEM((tok, half), bf),
                dma((2 * len(BLOCKS) + 3,)), dma((len(BLOCKS),)),
            ],
            compiler_params=pltpu.CompilerParams(vmem_limit_bytes=60 * 1024 * 1024),
        )(code, scale, post_gain, hidden, writing)

    placed = (
        P(("grp", "row"), "col"),
        P(("grp", "row"), "col"),
        P(("grp", "row"), "col"),
        P(("col", "row"), None),
        P("col"),
        P("col"),
        P("col", None),
        P("col", None),
    )
    return jax.shard_map(
        on_device, mesh=mesh, in_specs=placed, out_specs=P(("grp", "row"), "col"), check_vma=False
    )
```

```python
import functools

import jax
import jax.numpy as jnp
import numpy as np
from jax import lax
from jax.experimental import pallas as pl
from jax.experimental.pallas import tpu as pltpu
from jax.sharding import PartitionSpec as P

HD = 128
WINDOW = 1024
MESH = pl.DeviceIdType.MESH
query_scale = 168.0 ** (-0.5)
norm_eps = 1e-06
rope_base = 10000.0
QB = 256
BLOCKS = (384, 768, 1024, 512)
BIG = 1e30

CHUNKS = (("own", 128), ("pair", 512), ("pair", 256), ("pair", 256), ("pair", 256))
VIA_Z = (0, 3, 4)
ORDER = (
    ("kvup", 2), ("kvup", 3), ("kvup", 1), ("kvy", 2), ("kvup", 0), ("kvy", 3), ("own", 1), ("own", 2), ("tables",),
    ("line", 1, 1), ("kvrelay", 2), ("prep",), ("kvy", 1), ("line", 2, 1), ("rotk", 2), ("kvrelay", 3), ("G", 2),
    ("rotk", 3), ("att", 2), ("kvy", 0), ("cross", 1, 0), ("kvrelay", 1), ("G", 3), ("kvrelay", 0), ("att", 3),
    ("rotk", 1), ("line", 1, -1), ("line", 1, 2), ("own", 3), ("cross", 2, 0), ("G", 1), ("att", 1), ("rotk", 0),
    ("G", 0), ("line", 1, -2), ("own", 0), ("att", 0), ("line", 3, 1), ("attfwd", 1), ("line", 1, -3),
    ("line", 3, -1), ("line", 1, 3), ("line", 2, -1), ("line", 0, 1), ("own", 4), ("attfwd", 2), ("line", 2, 2),
    ("attfwd", 3), ("attfwd", 0), ("line", 3, 2), ("line", 2, -2), ("mm", 1), ("line", 2, -3), ("line", 3, -2),
    ("line", 4, 1), ("line", 4, -1), ("cross", 3, 0), ("line", 3, -3), ("line", 2, 3), ("line", 3, 3), ("line", 4, 2),
    ("line", 4, -2), ("line", 0, 2), ("line", 0, -1), ("cross", 4, 0), ("cross", 0, 0), ("mm", 2), ("hid", 1),
    ("line", 4, -3), ("line", 4, 3), ("mm", 3), ("line", 0, 3), ("line", 0, -2), ("mm", 4), ("hid", 3),
    ("line", 0, -3), ("hid", 2), ("mm", 0), ("drain",), ("hid", 4),
)


def plain_order(kinds, nz, kvh):
    n_chunk = len(kinds)
    out = [("own", k) for k in range(n_chunk)]
    out += [(a, h) for h in range(kvh) for a in ("kvup", "kvy")]
    out += [("tables",), ("prep",)]
    out += [("kvrelay", h) for h in range(kvh)]
    for k in range(n_chunk):
        for d in range(1, nz):
            out += [("line", k, -d), ("line", k, d)]
        out += [("cross", k, 0)]
        if kinds[k] == "both":
            out += [("cross", k, d) for e in range(1, nz) for d in (-e, e)]
    for p in range(kvh):
        out += [("rotk", p), ("G", p), ("att", p)]
    out += [("attfwd", p) for p in range(kvh)]
    out += [("mm", k) for k in range(n_chunk)]
    out += [("hid", k) for k in range(n_chunk) if kinds[k] == "pair"]
    return out


def split_cat(x):
    hi = x.astype(jnp.bfloat16).astype(jnp.float32)
    return jnp.concatenate([hi, x - hi], axis=0).astype(jnp.bfloat16)


def hi_lo(x):
    hi = x.astype(jnp.bfloat16)
    return hi, (x - hi.astype(jnp.float32)).astype(jnp.bfloat16)


def dot_nt(x, y):
    return lax.dot_general(x, y, (((1,), (1,)), ((), ())), preferred_element_type=jnp.float32)


def plan(n_row):
    nz = n_row // 2
    chunks = CHUNKS if nz == 4 else (("both", 384), ("pair", 1152))
    via_z = VIA_Z if nz == 4 else (0,)
    kinds = [c[0] for c in chunks]
    width = [c[1] for c in chunks]
    off, pair_w, rest_w = [], 0, 0
    for kind, w in chunks:
        off.append(pair_w if kind == "pair" else rest_w)
        pair_w, rest_w = (pair_w + w, rest_w) if kind == "pair" else (pair_w, rest_w + w)
    return kinds, width, off, pair_w, rest_w, via_z


def kernel(n_row, d_full, n_ss, q_hbm, k_hbm, v_hbm, w_hbm, *rest):
    params_hbm, rest = rest[:5], rest[5:]
    hid_out, eout_out, c_ref, scale_ref, *scratch = rest
    kinds, width, off, pair_w, rest_w, via_z = plan(n_row)
    n_chunk = len(kinds)
    pair, both = [c == "pair" for c in kinds], [c == "both" for c in kinds]
    wb = scratch[:n_chunk]
    (qbuf, kbuf, vbuf, krot, att, hid, hsend, cosb, sinb, ein_cat, eout_cat, code_acc, sq_acc, st_send, st_recv,
     gain_ref, mean_ref, ein_ref, eout_ref, inv_ref, loc_sem, ss_sem, wr_sem, xr_sem, cr_sem, kr_sem, ar_sem, hr_sem, st_sem, out_sem) = scratch[n_chunk:]
    nz = n_row // 2
    g, r, f = lax.axis_index("grp"), lax.axis_index("row"), lax.axis_index("col")
    zz, yy = r // 2, r % 2
    has_up, has_dn = zz < nz - 1, zz > 0
    tok = qbuf.shape[0]
    half = pair_w * 2 + rest_w
    kvh = kbuf.shape[0]
    heads = qbuf.shape[1] // HD
    acols = heads * HD
    per = tok // QB

    part = {"grp": g, "row": r, "col": 1 - f}
    xnb = {"grp": 1 - g, "row": r, "col": f}
    ynb = {"grp": g, "row": 2 * zz + 1 - yy, "col": f}
    up = {"grp": g, "row": r + 2, "col": f}
    dn = {"grp": g, "row": r - 2, "col": f}

    barrier = pltpu.get_barrier_semaphore()
    for nb in (part, xnb, ynb):
        pl.semaphore_signal(barrier, inc=1, device_id=nb, device_id_type=MESH)

    @pl.when(has_up)
    def _():
        pl.semaphore_signal(barrier, inc=1, device_id=up, device_id_type=MESH)

    @pl.when(has_dn)
    def _():
        pl.semaphore_signal(barrier, inc=1, device_id=dn, device_id_type=MESH)

    def own_w(k, c):
        at = c * half + (g * pair_w + off[k] if pair[k] else 2 * pair_w + off[k])
        return w_hbm.at[:, pl.ds(pl.multiple_of(at, 128), width[k])]

    def head_cols(h):
        return pl.ds(h * HD, HD)

    own_rows = pl.ds(2 * tok, tok)
    loc_w = [pltpu.make_async_copy(own_w(k, f), wb[k].at[f, r], loc_sem.at[k]) for k in range(n_chunk)]
    loc_k = [pltpu.make_async_copy(k_hbm.at[:, head_cols(h)], kbuf.at[h, own_rows, :], loc_sem.at[n_chunk + h])
             for h in range(kvh)]
    loc_v = [pltpu.make_async_copy(v_hbm.at[:, head_cols(h)], vbuf.at[h, own_rows, :], loc_sem.at[n_chunk + kvh + h])
             for h in range(kvh)]
    loc_q = pltpu.make_async_copy(q_hbm, qbuf, loc_sem.at[n_chunk + 2 * kvh])
    loc_p = [pltpu.make_async_copy(src, dst, loc_sem.at[n_chunk + 2 * kvh + 1 + i]) for i, (src, dst) in enumerate(
        zip(params_hbm, (gain_ref, mean_ref, ein_ref, eout_ref, inv_ref)))]
    for c in loc_w + loc_k + loc_v + [loc_q] + loc_p:
        c.start()

    pl.semaphore_wait(barrier, 3 + has_up.astype(jnp.int32) + has_dn.astype(jnp.int32))

    pending = []
    left = []

    def leave(src, dst):
        c = pltpu.make_async_copy(src, dst, out_sem.at[len(left)])
        left.append(c)
        c.start()

    def send(cond, dev, ends, *args):
        i = len(pending)
        assert i < n_ss, i

        def make():
            src, dst, recv = ends(*args)
            return pltpu.make_async_remote_copy(
                src_ref=src, dst_ref=dst, send_sem=ss_sem.at[i], recv_sem=recv, device_id=dev, device_id_type=MESH)

        pending.append((cond, make))
        if cond is None:
            make().start()
        else:
            @pl.when(cond)
            def _():
                make().start()

    def when(cond, fn):
        if cond is None:
            fn()
        else:
            pl.when(cond)(fn)

    def arrived(ref, sem):
        pltpu.make_async_copy(ref, ref, sem).wait()

    for k in range(n_chunk):
        send(None, part, lambda k: (own_w(k, 1 - f), wb[k].at[f, r], cr_sem.at[k]), k)

    def block(k, u):
        return wb[k].at[g, u] if both[k] else wb[k].at[:, u]

    def send_w(cond, k, u, dev):
        send(cond, dev, lambda: (block(k, u), block(k, u), wr_sem.at[k, u]))

    def send_x(cond, k, u):
        send(cond, xnb, lambda: (wb[k].at[g, u], wb[k].at[g, u], xr_sem.at[k, u]))

    def act_own(k):
        loc_w[k].wait()
        arrived(wb[k].at[1 - f, r], cr_sem.at[k])
        send_w(has_up, k, r, up)
        send_w(has_dn, k, r, dn)
        send_w(None, k, r, ynb)

    def inside(dz):
        return None if dz == 0 else (zz + dz >= 0 if dz < 0 else zz + dz < nz)

    def act_line(k, dz):
        cond, u = inside(dz), r + 2 * dz
        when(cond, lambda: arrived(block(k, u), wr_sem.at[k, u]))
        if dz < 0:
            send_w(cond & has_up, k, u, up)
        else:
            send_w(cond & has_dn, k, u, dn)
        if dz != 1:
            send_w(cond & has_up if dz == -1 and k in via_z else cond, k, u, ynb)
        if both[k]:
            send_x(cond, k, u)

    def act_cross(k, dz):
        cond, u = inside(dz), 2 * (zz + dz) + 1 - yy
        when(cond, lambda: arrived(block(k, u), wr_sem.at[k, u]))
        if dz == 0:
            send_w(has_dn, k, u, dn)
            if k in via_z:
                send_w(zz == nz - 2, k, u, up)
        if both[k]:
            send_x(cond, k, u)

    def kv_rows(slot):
        return pl.ds(slot * tok, tok)

    def send_kv(cond, h, src_slot, slot, dev):
        def ends(n):
            hbm, buf = ((k_hbm, kbuf), (v_hbm, vbuf))[n]
            src = hbm.at[:, head_cols(h)] if src_slot == 2 else buf.at[h, kv_rows(src_slot), :]
            return src, buf.at[h, kv_rows(slot), :], kr_sem.at[slot, h, n]

        for n in range(2):
            send(cond, dev, ends, n)

    def wait_kv(cond, h, slot):
        @pl.when(cond)
        def _():
            for n, buf in enumerate((kbuf, vbuf)):
                arrived(buf.at[h, kv_rows(slot), :], kr_sem.at[slot, h, n])

    def act_kvup(h):
        send_kv(has_up, h, 2, 0, up)

    def act_kvy(h):
        send_kv(yy == 0, h, 2, 1, ynb)

    def act_kvrelay(h):
        wait_kv(has_dn, h, 0)
        send_kv(has_dn & (yy == 1), h, 0, 1, ynb)

    sign = jnp.where(lax.broadcasted_iota(jnp.int32, (1, HD), 1) < HD // 2, -1.0, 1.0)
    key_base = r * tok - 2 * tok

    def table(i, _):
        at = pl.multiple_of(i * 128, 128)
        pos = (key_base + at + lax.broadcasted_iota(jnp.int32, (128, HD), 0)).astype(jnp.float32)
        ang = pos * inv_ref[...]
        cosb[pl.ds(at, 128), :] = jnp.cos(ang)
        sinb[pl.ds(at, 128), :] = jnp.sin(ang) * sign
        return 0

    def turned(x, at):
        x = x.astype(jnp.float32)
        cs, sn = cosb[pl.ds(at, 128), :], sinb[pl.ds(at, 128), :]
        return (x * cs + pltpu.roll(x, HD // 2, 1) * sn).astype(jnp.bfloat16)

    def rot_q(i, _):
        at = pl.multiple_of(i * 128, 128)
        for h in range(heads):
            cols = slice(h * HD, (h + 1) * HD)
            qbuf[pl.ds(at, 128), cols] = turned(qbuf[pl.ds(at, 128), cols], 2 * tok + at)
        return 0

    def rot_own(i, _):
        at = pl.multiple_of(2 * tok + i * 128, 128)
        for h in range(kvh):
            krot[h, pl.ds(at, 128), :] = turned(kbuf[h, pl.ds(at, 128), :], at)
        return 0

    def act_tables():
        @pl.when(zz == 0)
        def _():
            kbuf[:, kv_rows(0), :] = jnp.zeros((kvh, tok, HD), kbuf.dtype)
            vbuf[:, kv_rows(0), :] = jnp.zeros((kvh, tok, HD), vbuf.dtype)

        @pl.when(r == 0)
        def _():
            kbuf[:, kv_rows(1), :] = jnp.zeros((kvh, tok, HD), kbuf.dtype)
            vbuf[:, kv_rows(1), :] = jnp.zeros((kvh, tok, HD), vbuf.dtype)

        for c in loc_p:
            c.wait()
        lax.fori_loop(0, 3 * tok // 128, table, 0)

    def prep(i, m_acc):
        cols = pl.ds(pl.multiple_of(i * 384, 128), 384)
        e = ein_ref[:, cols]
        ein_cat[:, cols] = split_cat(e * gain_ref[cols][None, :])
        e = split_cat(e)
        m_hi, m_lo = hi_lo(jnp.broadcast_to(mean_ref[cols][None, :], (16, 384)))
        m_acc = m_acc + dot_nt(m_hi, e) + dot_nt(m_lo, e)
        eout_cat[:, cols] = split_cat(eout_ref[:, cols])
        return m_acc

    def act_prep():
        loc_q.wait()
        lax.fori_loop(0, tok // 128, rot_q, 0)
        for c in loc_k + loc_v:
            c.wait()
        lax.fori_loop(0, tok // 128, rot_own, 0)
        m_acc = lax.fori_loop(0, half // 384, prep, jnp.zeros((16, HD), jnp.float32))
        leave(eout_cat, eout_out)
        st_send[tok:tok + 8, :] = (m_acc + pltpu.roll(m_acc, HD // 2, 1))[0:8]
        code_acc[...] = jnp.zeros_like(code_acc)
        sq_acc[...] = jnp.zeros_like(sq_acc)

    def act_rotk(h):
        wait_kv(r > 0, h, 1)

        def body(i, _):
            at = pl.multiple_of(i * 128, 128)
            krot[h, pl.ds(at, 128), :] = turned(kbuf[h, pl.ds(at, 128), :], at)
            return 0

        lax.fori_loop(0, 2 * tok // 128, body, 0)

    nt = WINDOW // QB + 1
    ri = lax.broadcasted_iota(jnp.int32, (QB, QB), 0)
    ci = lax.broadcasted_iota(jnp.int32, (QB, QB), 1)
    pen = [jnp.where(zz > 0, 0.0, BIG), jnp.where(r > 0, 0.0, BIG), jnp.float32(0.0)]

    def act_G(kv):
        def piece(j, _):
            head, i = (heads // kvh) * kv + j // per, j % per
            rows = pl.ds(pl.multiple_of(i * QB, QB), QB)
            qt = qbuf[rows, pl.ds(pl.multiple_of(head * HD, HD), HD)]
            key_rows = pl.ds(pl.multiple_of(i * QB, QB), nt * QB)
            s = dot_nt(qt, krot[kv, key_rows, :]) * query_scale
            tiles, bias, m = [], [], None
            for t in range(nt):
                st = s[:, t * QB:(t + 1) * QB]
                if t == 0:
                    st = jnp.where(ci > ri, st, -BIG)
                if t == nt - 1:
                    st = jnp.where(ci <= ri, st, -BIG)
                blk = (i + t) // per
                b = jnp.where(blk == 0, pen[0], jnp.where(blk == 1, pen[1], pen[2]))
                mt = jnp.max(st, axis=1, keepdims=True) - b
                m = mt if m is None else jnp.maximum(m, mt)
                tiles.append(st)
                bias.append(b)
            es, tot = [], None
            for st, b in zip(tiles, bias):
                e = jnp.exp(st - (m + b))
                es.append(e)
                se = jnp.sum(e, axis=1, keepdims=True)
                tot = se if tot is None else tot + se
            inv = 1.0 / tot
            p = jnp.concatenate([(e * inv).astype(jnp.bfloat16) for e in es], axis=1)
            o = jnp.dot(p, vbuf[kv, key_rows, :], preferred_element_type=jnp.float32)
            att[rows, pl.ds(pl.multiple_of(f * acols + head * HD, HD), HD)] = o.astype(jnp.bfloat16)
            return 0

        lax.fori_loop(0, (heads // kvh) * per, piece, 0)

    group = heads // kvh * HD
    mine, other = pl.ds(0, tok), pl.ds(tok, tok)

    def att_cols(c, p):
        return pl.ds(pl.multiple_of(c * acols + p * group, 128), group)

    def act_att(p):
        cols = att_cols(f, p)
        send(None, xnb, lambda: (att.at[mine, cols], att.at[other, cols], ar_sem.at[0, p]))
        send(None, part, lambda: (att.at[mine, cols], att.at[mine, cols], ar_sem.at[1, p]))

    def act_attfwd(p):
        cols = att_cols(f, p)
        arrived(att.at[other, cols], ar_sem.at[0, p])
        send(None, part, lambda: (att.at[other, cols], att.at[other, cols], ar_sem.at[2, p]))

    lane = lax.broadcasted_iota(jnp.int32, (tok, HD), 1)
    gained = [False, False]
    mark, drained = [0], [0]

    def hid_cols(k, c):
        return pl.ds(pl.multiple_of(c * pair_w + off[k], 128) if pair[k] else 2 * pair_w + off[k], width[k])

    def stats(k, c):
        cols, w = hid_cols(k, c), width[k]

        def body(i, _):
            rows = pl.ds(pl.multiple_of(i * QB, QB), QB)
            h = hid[rows, cols]
            code_acc[rows, :] += dot_nt(h, ein_cat[:, cols])
            h = h.astype(jnp.float32)
            sq = sq_acc[rows, :]
            for t in range(w // HD):
                ht = h[:, t * HD:(t + 1) * HD]
                sq = sq + ht * ht
            sq_acc[rows, :] = sq
            return 0

        leave(hid.at[:, cols], hid_out.at[:, cols])
        lax.fori_loop(0, per, body, 0)

    def act_mm(k):
        mark[0] = len(pending)
        if not gained[0]:
            gained[0] = True
            for p in range(kvh):
                arrived(att.at[mine, att_cols(1 - f, p)], ar_sem.at[1, p])
        if pair[k] and not gained[1]:
            gained[1] = True
            for p in range(kvh):
                arrived(att.at[other, att_cols(1 - f, p)], ar_sem.at[2, p])
        if both[k]:
            for dz in range(1 - nz, nz):
                for u, skip in ((r + 2 * dz, dz == 0), (2 * (zz + dz) + 1 - yy, False)):
                    if not skip:
                        when(inside(dz), lambda: arrived(wb[k].at[1 - g, u], xr_sem.at[k, u]))
        else:
            for dz in range(1 - nz, nz):
                if dz != 0:
                    act_cross(k, dz)
        wk = wb[k].reshape(2 * acols, width[k])

        def product(at):
            return jnp.dot(att[pl.ds(pl.multiple_of(at, QB), QB), :], wk[...], preferred_element_type=jnp.float32)

        if not pair[k]:
            whole = jnp.dot(att[mine, :], wk[...], preferred_element_type=jnp.float32)
            hid[:, hid_cols(k, g)] = whole.astype(jnp.bfloat16)
            stats(k, g)
        else:
            cols = slice(off[k], off[k] + width[k])

            def body(i, _):
                n = jnp.where(i < per, i, i - per)
                at = pl.multiple_of(n * QB, QB)
                d = product(jnp.where(i < per, tok, 0) + at).astype(jnp.bfloat16)

                @pl.when(i < per)
                def _():
                    hsend[pl.ds(at, QB), cols] = d

                def ends(j):
                    rows = pl.ds(j * QB, QB)
                    return hsend.at[rows, cols], hid.at[rows, hid_cols(k, g)], hr_sem.at[k, j]

                for j in range(per):
                    send(i == j, xnb, ends, j)
                    pending[-1] = (None, pending[-1][1])

                @pl.when(i >= per)
                def _():
                    hid[pl.ds(at, QB), hid_cols(k, g)] = d
                return 0

            lax.fori_loop(0, 2 * per, body, 0)
            stats(k, g)

    def act_hid(k):
        for j in range(per):
            arrived(hid.at[pl.ds(j * QB, QB), hid_cols(k, 1 - g)], hr_sem.at[k, j])
        stats(k, 1 - g)

    def drain(end):
        for cond, make in pending[drained[0]:end]:
            when(cond, lambda make=make: make().wait_send())
        drained[0] = end

    def act_drain():
        drain(mark[0])

    acts = {"drain": act_drain, "own": act_own, "line": act_line, "cross": act_cross, "kvup": act_kvup, "kvy": act_kvy,
            "kvrelay": act_kvrelay, "tables": act_tables, "prep": act_prep, "rotk": act_rotk, "G": act_G,
            "att": act_att, "attfwd": act_attfwd, "mm": act_mm, "hid": act_hid}
    for name, *rest in ORDER if nz == 4 else plain_order(kinds, nz, kvh):
        acts[name](*rest)

    code = code_acc[...]
    code = code + pltpu.roll(code, HD // 2, 1)
    sq = jnp.sum(sq_acc[...], axis=1, keepdims=True)
    st_send[0:tok, :] = jnp.where(lane < HD // 2, code, sq)
    swap = pltpu.make_async_remote_copy(src_ref=st_send, dst_ref=st_recv, send_sem=st_sem.at[0], recv_sem=st_sem.at[1],
                                        device_id=part, device_id_type=MESH)
    swap.start()
    drain(len(pending))
    swap.wait()
    sums = st_send[0:tok, :] + st_recv[0:tok, :]
    turned_sums = pltpu.roll(sums, HD // 2, 1)
    code = jnp.where(lane < HD // 2, sums, turned_sums)
    total = jnp.where(lane < HD // 2, turned_sums, sums)
    inv_rms = lax.rsqrt(total * (1.0 / d_full) + norm_eps)
    mean_sum = st_send[tok:tok + 1, :] + st_recv[tok:tok + 1, :]
    c_hi, c_lo = hi_lo(inv_rms * code - mean_sum)
    c_ref[:, 0:HD] = c_hi
    c_ref[:, HD:2 * HD] = c_lo
    scale_ref[...] = inv_rms
    for c in left:
        c.wait()


def finish(c_hbm, scale_hbm, gain_hbm, hid_hbm, eout_hbm, out_hbm, c_ref, scale_ref, gain_ref, hid, eout, out, in_sem,
           out_sem):
    n = len(BLOCKS)

    def cols(i):
        return pl.ds(sum(BLOCKS[:i]), BLOCKS[i])

    def come(i):
        return (pltpu.make_async_copy(eout_hbm.at[:, cols(i)], eout.at[:, cols(i)], in_sem.at[i]),
                pltpu.make_async_copy(hid_hbm.at[:, cols(i)], hid.at[:, cols(i)], in_sem.at[n + i]))

    def go(i):
        return pltpu.make_async_copy(out.at[:, cols(i)], out_hbm.at[:, cols(i)], out_sem.at[i])

    first = [pltpu.make_async_copy(src, dst, in_sem.at[2 * n + j]) for j, (src, dst) in enumerate(
        ((c_hbm, c_ref), (scale_hbm, scale_ref), (gain_hbm, gain_ref)))]
    for c in first:
        c.start()
    for i in range(n):
        for c in come(i):
            c.start()
    for c in first:
        c.wait()

    def body(i):
        for c in come(i):
            c.wait()
        e = eout[:, cols(i)]
        back = jnp.dot(c_ref[...], jnp.concatenate([e, e], axis=0), preferred_element_type=jnp.float32)
        h = hid[:, cols(i)].astype(jnp.float32) * jnp.concatenate([scale_ref[...]] * (BLOCKS[i] // HD), axis=1)
        out[:, cols(i)] = (h * gain_ref[cols(i)][None, :] - back).astype(jnp.bfloat16)
        go(i).start()

    for i in range(n):
        body(i)
    for i in range(n):
        go(i).wait()


def solution(mesh):
    n_row = mesh.shape["row"]

    def on_device(queries, keys, values, out_proj, post_gain, mean_vec, erase_in, erase_out):
        tok = queries.shape[0]
        rows, d_full = out_proj.shape
        half = post_gain.shape[0]
        half_dim = HD // 2
        kvh = keys.shape[1] // HD
        inverse = np.exp(-(2.0 * np.arange(half_dim, dtype=np.float32) / HD) * np.log(np.float32(rope_base)))
        inverse = np.concatenate([inverse, inverse]).astype(np.float32)[None, :]
        any_spec = pl.BlockSpec(memory_space=pltpu.HBM)
        vm = pl.BlockSpec(memory_space=pltpu.VMEM)
        kinds, width, off, pair_w, rest_w, via_z = plan(n_row)
        n_chunk = len(kinds)
        hops = n_row // 2 - 1
        n_ss = sum(6 + 4 * hops + (b == "both") * (4 * hops + 1) + tok // QB for b in kinds) + 9 * kvh
        bf, f32 = jnp.bfloat16, jnp.float32
        dma = pltpu.SemaphoreType.DMA
        hidden, writing, code, scale = pl.pallas_call(
            functools.partial(kernel, n_row, d_full, n_ss),
            out_shape=[jax.ShapeDtypeStruct((tok, half), bf), jax.ShapeDtypeStruct((HD, half), bf),
                       jax.ShapeDtypeStruct((tok, 2 * HD), bf), jax.ShapeDtypeStruct((tok, HD), f32)],
            in_specs=[any_spec] * 9,
            out_specs=[pl.BlockSpec(memory_space=pl.ANY)] * 2 + [vm, vm],
            scratch_shapes=[pltpu.VMEM((2, n_row, rows, w), bf) for w in width] + [
                pltpu.VMEM(queries.shape, bf),
                pltpu.VMEM((kvh, 3 * tok, HD), bf),
                pltpu.VMEM((kvh, 3 * tok, HD), bf),
                pltpu.VMEM((kvh, 3 * tok, HD), bf),
                pltpu.VMEM((2 * tok, 2 * queries.shape[1]), bf),
                pltpu.VMEM((tok, half), bf),
                pltpu.VMEM((tok, pair_w), bf),
                pltpu.VMEM((3 * tok, HD), f32),
                pltpu.VMEM((3 * tok, HD), f32),
                pltpu.VMEM((HD, half), bf),
                pltpu.VMEM((HD, half), bf),
                pltpu.VMEM((tok, HD), f32),
                pltpu.VMEM((tok, HD), f32),
                pltpu.VMEM((tok + 8, HD), f32),
                pltpu.VMEM((tok + 8, HD), f32),
                pltpu.VMEM((half,), f32),
                pltpu.VMEM((half,), f32),
                pltpu.VMEM((erase_in.shape[1], half), f32),
                pltpu.VMEM((erase_in.shape[1], half), f32),
                pltpu.VMEM((1, HD), f32),
                dma((n_chunk + 2 * kvh + 6,)), dma((n_ss,)), dma((n_chunk, n_row)), dma((n_chunk, n_row)),
                dma((n_chunk,)), dma((2, kvh, 2)), dma((3, kvh)), dma((n_chunk, tok // QB)), dma((2,)),
                dma((1 + sum(2 if b == "pair" else 1 for b in kinds),)),
            ],
            compiler_params=pltpu.CompilerParams(
                collective_id=0, has_side_effects=True, vmem_limit_bytes=60 * 1024 * 1024),
        )(queries, keys, values, out_proj, post_gain, mean_vec,
          erase_in.T, erase_out.T, jnp.asarray(inverse))
        return pl.pallas_call(
            finish,
            out_shape=jax.ShapeDtypeStruct((tok, half), bf),
            in_specs=[any_spec] * 5,
            out_specs=any_spec,
            scratch_shapes=[
                pltpu.VMEM((tok, 2 * HD), bf), pltpu.VMEM((tok, HD), f32), pltpu.VMEM((half,), f32),
                pltpu.VMEM((tok, half), bf), pltpu.VMEM((HD, half), bf), pltpu.VMEM((tok, half), bf),
                dma((2 * len(BLOCKS) + 3,)), dma((len(BLOCKS),)),
            ],
            compiler_params=pltpu.CompilerParams(vmem_limit_bytes=60 * 1024 * 1024),
        )(code, scale, post_gain, hidden, writing)

    placed = (
        P(("grp", "row"), "col"),
        P(("grp", "row"), "col"),
        P(("grp", "row"), "col"),
        P(("col", "row"), None),
        P("col"),
        P("col"),
        P("col", None),
        P("col", None),
    )
    return jax.shard_map(
        on_device, mesh=mesh, in_specs=placed, out_specs=P(("grp", "row"), "col"), check_vma=False
    )
```
